32 devices in a mesh: loop: 16 (over z, x, core), team: 2 (over y).
Axes of the slice: x: 2, y: 2, z: 4, core: 2. Of those that a mesh axis runs over, the one named last changes fastest.
Arguments:
- blocks: bfloat16 [4096, 128, 128], P(('loop', 'team')), may hold values from -0.078125 to 0.078125
- probes: bfloat16 [32768, 128], P(('loop', 'team')), may hold values from -6 to 6
- row_count: int32 [64], P(('loop', 'team')), may hold values from 0 to 64, as said below
- column_of_slot: int32 [4096], P(('loop', 'team')), may hold values from 0 to 255, as said below
Outputs:
- sketch: float32 [8192, 128], P(('loop', 'team'))
The draws below stay inside these ranges and needn't reach their ends.
Inputs may be any that keep to these rules, and one draw needn't show every extreme that they name: `row_count`: A device's block rows hold 128 stored blocks or fewer together, and some device holds exactly 128; each block row holds at most min(64, 128), some block row exactly that many, and some block row none. `column_of_slot`: A used slot of a device in loop position t holds a block column in the pieces of loop indices t, t-1, ..., t-3 (mod 16), piece p covering block columns p * 16 to p * 16 + 15; columns within one block row are distinct. Unused slots hold columns of the same range.
All inputs are finite; a program needn't handle non-finite values.
Results may differ from the reference program's by a relative error of at most 0.0003.
Values may be sent and summed in bfloat16 or wider, within the bound.
A program may use at most 64 MiB of HBM per device.

```python
import jax
import jax.numpy as jnp
from jax import lax

BLOCK_EDGE = 128
PROBES = 128
CB = 16
RB = 2
DEVICE_SLOTS = 128
BLOCK_REACH = 64
CELLS = 32768
ROWS = 8192
TOTAL_SLOTS = 4096
N_LOOP = 16
DEVICES = 32


def pattern_helper(key):
    base = jax.random.fold_in(key, 7)
    key_overall = jax.random.fold_in(base, 1)
    key_full = jax.random.fold_in(base, 2)
    key_perm = jax.random.fold_in(base, 3)
    key_split = jax.random.fold_in(base, 4)
    device_numbers = jnp.arange(DEVICES, dtype=jnp.int32)
    running_sums = jax.random.randint(key_overall, (DEVICES,), DEVICE_SLOTS // 4, DEVICE_SLOTS + 1).astype(jnp.int32)
    device_filled = jax.random.randint(key_full, (), 0, DEVICES).astype(jnp.int32)
    empty_device = ((device_filled + 1) % DEVICES).astype(jnp.int32)
    running_sums = jnp.where(device_numbers == device_filled, DEVICE_SLOTS, running_sums)
    running_sums = jnp.where(device_numbers == empty_device, jnp.minimum(running_sums, BLOCK_REACH), running_sums).astype(jnp.int32)
    remain = running_sums
    count_list = []
    for row_number in range(RB - 1):
        rest_cap = (RB - 1 - row_number) * BLOCK_REACH
        low = jnp.maximum(0, remain - rest_cap)
        high = jnp.minimum(BLOCK_REACH, remain)
        part_key = jax.random.fold_in(key_split, row_number)
        selected_rows = jax.random.randint(part_key, (DEVICES,), low, high + 1).astype(jnp.int32)
        if row_number == 0:
            selected_rows = jnp.where(device_numbers == device_filled, min(BLOCK_REACH, DEVICE_SLOTS), selected_rows)
            selected_rows = jnp.where(device_numbers == empty_device, 0, selected_rows).astype(jnp.int32)
        count_list.append(selected_rows)
        remain = remain - selected_rows
    count_list.append(remain)
    counts = jnp.stack(count_list, axis=1).astype(jnp.int32)
    ends = jnp.cumsum(counts, axis=1).astype(jnp.int32)
    starts = (ends - counts).astype(jnp.int32)
    slot_entries = jnp.arange(DEVICE_SLOTS, dtype=jnp.int32)
    owner = jnp.sum((slot_entries[None, :, None] >= ends[:, None, :]).astype(jnp.int32), axis=2)
    owner_row = jnp.minimum(owner, RB - 1)
    start_of = jnp.take_along_axis(starts, owner_row, axis=1)
    rank = jnp.where(owner < RB, slot_entries[None, :] - start_of, slot_entries[None, :]) % BLOCK_REACH
    perm_keys = jax.random.split(key_perm, DEVICES * RB)
    perms = jax.vmap(lambda one_key: jax.random.permutation(one_key, BLOCK_REACH))(perm_keys)
    perms = perms.reshape(DEVICES, RB, BLOCK_REACH).astype(jnp.int32)
    flat_index = owner_row * BLOCK_REACH + rank
    position = jnp.take_along_axis(perms.reshape(DEVICES, RB * BLOCK_REACH), flat_index, axis=1)
    stop = position // CB
    within = position % CB
    team_count = DEVICES // N_LOOP
    loop_of = (device_numbers // team_count)[:, None]
    piece = (loop_of - stop) % N_LOOP
    column = (piece * CB + within).astype(jnp.int32)
    return (counts.reshape(-1), column.reshape(-1))


def draw_row_count(key, part):
    return pattern_helper(key)[0]


def draw_column_of_slot(key, part):
    return pattern_helper(key)[1]


def steps_of(own_key, dims, shards, low, largest):
    def one(dim, blocks):
        steps = jax.random.uniform(jax.random.fold_in(jax.random.fold_in(own_key, 6), dim), (blocks,), jnp.float32, low / len(shards), largest / len(shards))
        return jnp.repeat(jnp.exp(steps), dims[dim] // blocks).reshape((-1,) + (1,) * (len(dims) - dim - 1))

    loudness = one(*shards[0])
    for cut in shards[1:]:
        loudness = loudness * one(*cut)
    return loudness


def scatter_about(own_key, shape, width, most, cuts=(), held_as=jnp.bfloat16):
    gain = steps_of(own_key, shape, cuts, -0.22, 0.18) if cuts else 1.0
    array = jax.random.normal(own_key, shape, jnp.float32) * width * gain
    return jnp.minimum(jnp.maximum(array, -most), most).astype(held_as)


def setup_inputs(seed: int = 0) -> dict:
    keys = jax.random.split(jax.random.key(seed), 5)
    return {
        "blocks": scatter_about(keys[0], (TOTAL_SLOTS, BLOCK_EDGE, BLOCK_EDGE), (BLOCK_EDGE * DEVICE_SLOTS // 3) ** -0.5, 0.078125, ((0, 32),)),
        "probes": scatter_about(keys[1], (CELLS, PROBES), 1.0, 6.0, ((0, 32),)),
        "row_count": draw_row_count(jax.random.fold_in(keys[4], 71), 0),
        "column_of_slot": draw_column_of_slot(jax.random.fold_in(keys[4], 71), 0),
    }


def reference(blocks, probes, row_count, column_of_slot):
    omega = probes.reshape(CELLS // BLOCK_EDGE, BLOCK_EDGE, PROBES)
    stacked_blocks = blocks.reshape(DEVICES, DEVICE_SLOTS, BLOCK_EDGE, BLOCK_EDGE)
    column_list = column_of_slot.reshape(DEVICES, DEVICE_SLOTS)
    counts = row_count.reshape(DEVICES, RB)

    def one_device(items):
        block_set, column_set, count_set = items
        tiles = omega[column_set]
        prod = jnp.einsum("sij,sjk->sik", block_set.astype(jnp.float32), tiles.astype(jnp.float32))
        ends = jnp.cumsum(count_set).astype(jnp.int32)
        slot_entries = jnp.arange(DEVICE_SLOTS, dtype=jnp.int32)
        owner = jnp.sum((slot_entries[:, None] >= ends[None, :]).astype(jnp.int32), axis=1)
        onehot = (owner[None, :] == jnp.arange(RB, dtype=jnp.int32)[:, None]).astype(jnp.float32)
        summed = jnp.einsum("rs,sik->rik", onehot, prod, precision=lax.Precision.HIGHEST)
        return summed.reshape(RB * BLOCK_EDGE, PROBES)

    result = lax.map(one_device, (stacked_blocks, column_list, counts))
    return result.reshape(ROWS, PROBES)
```

```python
import functools

import jax
import jax.numpy as jnp
from jax import lax
from jax.experimental import pallas as pl
from jax.experimental.pallas import tpu as pltpu
from jax.sharding import PartitionSpec as P

STOPS = 4
LANES = 128


def div(x, n):
    return lax.shift_right_logical(x, n.bit_length() - 1) if n & (n - 1) == 0 else lax.div(x, n)


def rem(x, n):
    return x & (n - 1) if n & (n - 1) == 0 else lax.rem(x, n)


def kernel(geo, meta_ref, blocks_ref, probes_ref, out_ref,
           blk, win, inv_v, inv_s, recv, send, loc):
    loop_n, team_n, chunks, rows_here, slots, edge, tps = geo
    chunk = tps * edge // chunks
    per_chunk = tps // chunks
    per_piece = team_n * tps
    span = STOPS * per_piece
    mates = range(1, team_n)
    t = lax.axis_index("loop")
    m = lax.axis_index("team")
    core = lax.rem(t, 2)
    lower = core == 0
    upper = core == 1
    odd = lax.rem(lax.div(t, 2), 2) == 1
    even = ~odd
    wrap_in = t < 4
    wrap_out = t >= loop_n - 2

    def at(dt, dm):
        return {"loop": lax.rem(t + dt + loop_n, loop_n), "team": lax.rem(m + dm + team_n, team_n)}

    bulk = [
        pltpu.make_async_copy(probes_ref, win.at[0, 0], loc.at[0]),
        pltpu.make_async_copy(blocks_ref, blk.at[pl.ds(0, slots)], loc.at[1]),
    ]

    barrier = pltpu.get_barrier_semaphore()

    def greet(dt, dm):
        pl.semaphore_signal(barrier, inc=1, device_id=at(dt, dm), device_id_type=pl.DeviceIdType.MESH)

    greet(-3, 0)

    @pl.when(upper)
    def _():
        greet(-2, 0)
        for d in mates:
            greet(-1, d)
            greet(0, d)

    @pl.when(lower & odd)
    def _():
        pl.when(wrap_in)(lambda: greet(-1, 0))
        for d in mates:
            pl.when(~wrap_in)(lambda: greet(0, d))
    greet(1 - 2 * core, 0)

    for copy in bulk:
        copy.start()

    near_odd = (odd & ~wrap_in).astype(jnp.int32)
    far_even = (even & wrap_in).astype(jnp.int32)
    pl.semaphore_wait(barrier, jnp.where(
        lower, team_n + 1 + (team_n - 1) * near_odd, team_n + 2 + far_even))

    groups = []

    def rows(c):
        return pl.ds(c * chunk if isinstance(c, int) else pl.multiple_of(c * chunk, chunk), chunk)

    def group(only=None, size=chunks):
        groups.append((only, size))
        return len(groups) - 1

    def push(g, src, k, d, c, where, always=False):
        copy = pltpu.make_async_remote_copy(
            src_ref=src, dst_ref=win.at[k, d, rows(c)],
            send_sem=send.at[g], recv_sem=recv.at[k, d, c],
            device_id=where, device_id_type=pl.DeviceIdType.MESH)
        if always or groups[g][0] is None:
            copy.start()
        else:
            pl.when(groups[g][0])(copy.start)

    def finish(g):
        only, size = groups[g]

        def wait():
            ref = win.at[0, 0, pl.ds(0, size * chunk)]
            pltpu.make_async_copy(ref, ref, send.at[g]).wait()
        if only is None:
            wait()
        else:
            pl.when(only)(wait)

    def arrive(k, d, c):
        ref = win.at[k, d, rows(c)]
        pltpu.make_async_copy(ref, ref, recv.at[k, d, c]).wait()
        return ref

    backward = range(chunks - 1, -1, -1)
    g_ahead = group()
    g_mate = {d: group() for d in mates}
    g_third = group(lower | ~(odd & wrap_out))

    @pl.when(lower)
    def _():
        for c in range(chunks):
            push(g_ahead, probes_ref.at[rows(c)], 3, 0, c, at(3, 0))
            for d in mates:
                push(g_mate[d], probes_ref.at[rows(chunks - 1 - c)], 1, d, chunks - 1 - c, at(1, d))
            push(g_third, probes_ref.at[rows(c)], 1, 0, c, at(1, 0), True)

    @pl.when(upper)
    def _():
        for c in range(chunks):
            push(g_ahead, probes_ref.at[rows(c)], 2, 0, c, at(2, 0))
            for d in mates:
                push(g_mate[d], probes_ref.at[rows(chunks - 1 - c)], 0, d, chunks - 1 - c, at(0, d))
            push(g_third, probes_ref.at[rows(c)], 3, 0, c, at(3, 0))

    col = meta_ref[:, :slots]
    within = rem(col, per_piece)
    stop = rem(t - div(col, per_piece) + loop_n, loop_n)
    member = rem(m - div(within, tps) + team_n, team_n)
    key = (stop * team_n + member) * tps + rem(within, tps)
    number = lax.broadcasted_iota(jnp.int32, key.shape, 1)
    end = jnp.zeros((1, 1), jnp.int32)
    for r in range(rows_here):
        end = end + meta_ref[:, slots + r:slots + r + 1]
        key = key + jnp.where(number >= end, span, 0)
    key = jnp.where(number < end, key, -1)
    entries = inv_v.shape[1]
    keys = jnp.broadcast_to(key, (LANES, slots)).T[:, :1]
    hit = keys == lax.broadcasted_iota(jnp.int32, (slots, entries), 1)
    owner = jnp.where(hit, lax.broadcasted_iota(jnp.int32, (slots, entries), 0), slots)
    inv_v[...] = jnp.min(owner, axis=0, keepdims=True)
    inv_copy = pltpu.make_async_copy(inv_v, inv_s, loc.at[2])
    inv_copy.start()
    blk[slots] = jnp.zeros(blk.shape[1:], blk.dtype)
    inv_copy.wait()
    for copy in bulk:
        copy.wait()

    def compute(k, d, c=0, n=chunks, first=False):
        total = None
        step = 2 if (n * per_chunk) % 2 == 0 else 1
        for j in range(0, n * per_chunk, step):
            near = c * per_chunk + j
            base = (k * team_n + d) * tps + near
            left = []
            for r in range(rows_here):
                pair = [blk[inv_s[0, r * span + base + i]] for i in range(step)]
                left.append(jnp.concatenate(pair, axis=1))
            start = near * edge if isinstance(near, int) else pl.multiple_of(near * edge, edge)
            part = jnp.dot(jnp.concatenate(left, axis=0), win[k, d, pl.ds(start, step * edge)],
                           preferred_element_type=jnp.float32)
            total = part if total is None else total + part
        if first:
            out_ref[...] = total
        else:
            out_ref[...] += total

    def take(k, d):
        for c in range(chunks):
            arrive(k, d, c)
        compute(k, d)

    compute(0, 0, first=True)

    def relayed(c):
        return c >= chunks // 4, c >= chunks - max(1, chunks // 4)

    def either(on_even, on_odd):
        if on_even == on_odd:
            return None if on_even else False
        return even if on_even else odd

    def upper_core():
        g_low_mate = {d: group() for d in mates}
        g_low_piece = {k: group() for k in (2, 3)}
        g_low_far = {(k, d): group() for k in (2, 3) for d in mates}
        g_third_mate = {d: group(even | wrap_out) for d in mates}
        g_side = group(even & wrap_in)
        g_on = {(k, d, c): group(either(*relayed(c)), 1) for k in (2, 3) for d in mates for c in range(chunks)
                if either(*relayed(c)) is not False}
        g_over = {(k, d, c): group(either(*(not x for x in relayed(c)[::-1])), 1)
                  for k in (2, 3) for d in mates for c in range(chunks)
                  if either(*(not x for x in relayed(c)[::-1])) is not False}
        late = odd & wrap_out

        def mate(c):
            for d in mates:
                got = arrive(0, d, c)
                if (2, d, c) in g_on:
                    push(g_on[2, d, c], got, 2, d, c, at(2, 0))
                pl.when(even)(lambda: push(g_third_mate[d], got, 3, d, c, at(3, 0), True))
                got = arrive(1, d, c)
                if (3, d, c) in g_on:
                    push(g_on[3, d, c], got, 3, d, c, at(2, 0))
                push(g_low_mate[d], got, 0, d, c, at(-1, 0))

        def piece(k, c):
            got = arrive(k, 0, c)
            for d in mates:
                if (k, d, c) in g_over:
                    push(g_over[k, d, c], got, k, d, c, at(0, d))
            push(g_low_piece[k], got, k - 1, 0, c, at(-1, 0))
            if k == 2:
                push(g_side, got, 3, 0, c, at(1, 0))

        def far(k, d, c):
            got = arrive(k, d, c)
            push(g_low_far[k, d], got, k - 1, d, c, at(-1, 0))

        take(1, 0)
        for c in backward:
            mate(c)
        for d in mates:
            @pl.when(late)
            def _():
                if d == 1:
                    finish(g_ahead)
                for c in backward:
                    push(g_third_mate[d], win.at[0, d, rows(c)], 3, d, c, at(3, 0), True)
            compute(0, d)
            compute(1, d)

        @pl.when(~(even & wrap_in))
        def _():
            for c in range(chunks):
                for k in (3, 2):
                    piece(k, c)
                    compute(k, 0, c, 1)
            for i in range(chunks):
                c = 0 if i == 0 else jnp.where(odd, chunks - i, i)
                for d in mates:
                    for k in (3, 2):
                        far(k, d, c)
                        compute(k, d, c, 1)

        @pl.when(even & wrap_in)
        def _():
            for s in range(chunks + 2):
                if s < chunks:
                    for k in (3, 2):
                        piece(k, s)
                        compute(k, 0, s, 1)
                if s >= 2:
                    for d in mates:
                        for k in (3, 2):
                            far(k, d, s - 2)
                            compute(k, d, s - 2, 1)

    def lower_core():
        g_three = {d: group(odd & ~wrap_in) for d in mates}

        def mate():
            for d in mates:
                for c in backward:
                    arrive(0, d, c)
                compute(0, d)

        def third(forward):
            for c in range(chunks):
                got = arrive(3, 0, c)
                if forward:
                    for d in mates:
                        push(g_three[d], got, 3, d, c, at(0, d))
            compute(3, 0)

        def third_mate():
            for d in mates:
                for c in backward:
                    arrive(3, d, c)
                compute(3, d)

        def pieces():
            for c in range(chunks):
                for k in (2, 1):
                    arrive(k, 0, c)
                    compute(k, 0, c, 1)

        def fars():
            for i in range(chunks):
                c = 0 if i == 0 else jnp.where(odd, chunks - i, i)
                for d in mates:
                    for k in (2, 1):
                        arrive(k, d, c)
                        compute(k, d, c, 1)

        mate()

        @pl.when(~wrap_in)
        def _():
            third(True)
            pieces()
            third_mate()
            fars()

        @pl.when(wrap_in & odd)
        def _():
            pieces()
            fars()
            third(False)
            third_mate()

        @pl.when(wrap_in & even)
        def _():
            for s in range(chunks + 2):
                if s < chunks:
                    arrive(3, 0, s)
                    compute(3, 0, s, 1)
                    for k in (2, 1):
                        arrive(k, 0, s)
                        compute(k, 0, s, 1)
                for d in mates:
                    if 1 <= s <= chunks:
                        arrive(3, d, chunks - s)
                        compute(3, d, chunks - s, 1)
                    if s >= 2:
                        for k in (2, 1):
                            arrive(k, d, s - 2)
                            compute(k, d, s - 2, 1)

    def role(body):
        mark = len(groups)
        body()
        for g in range(mark, len(groups)):
            finish(g)
        del groups[mark:]

    pl.when(upper)(lambda: role(upper_core))
    pl.when(lower)(lambda: role(lower_core))

    @pl.when(lower | ~(odd & wrap_out))
    def _():
        finish(g_ahead)
    for d in mates:
        finish(g_mate[d])
    finish(g_third)


def sends(team_n, chunks):
    mates = team_n - 1
    return 5 + mates * (5 + 4 * chunks)


def local(loop_n, team_n, blocks, probes, row_count, column_of_slot):
    slots, edge, _ = blocks.shape
    width = probes.shape[1]
    tps = probes.shape[0] // edge
    rows_here = row_count.shape[0]
    chunks = min(4, tps)
    geo = (loop_n, team_n, chunks, rows_here, slots, edge, tps)
    entries = rows_here * STOPS * team_n * tps
    table = (1, -(-entries // LANES) * LANES)
    meta = jnp.concatenate([column_of_slot, row_count]).reshape(1, slots + rows_here)
    return pl.pallas_call(
        functools.partial(kernel, geo),
        out_shape=jax.ShapeDtypeStruct((rows_here * edge, width), jnp.float32),
        in_specs=[
            pl.BlockSpec(memory_space=pltpu.VMEM),
            pl.BlockSpec(memory_space=pltpu.HBM),
            pl.BlockSpec(memory_space=pltpu.HBM),
        ],
        out_specs=pl.BlockSpec(memory_space=pltpu.VMEM),
        scratch_shapes=[
            pltpu.VMEM((slots + 1, edge, edge), blocks.dtype),
            pltpu.VMEM((STOPS, team_n, tps * edge, width), probes.dtype),
            pltpu.VMEM(table, jnp.int32),
            pltpu.SMEM(table, jnp.int32),
            pltpu.SemaphoreType.DMA((STOPS, team_n, chunks)),
            pltpu.SemaphoreType.DMA((sends(team_n, chunks),)),
            pltpu.SemaphoreType.DMA((3,)),
        ],
        compiler_params=pltpu.CompilerParams(
            collective_id=0, has_side_effects=True, vmem_limit_bytes=55000 * 1024),
    )(meta, blocks, probes)


def solution(mesh):
    spec = ("loop", "team")
    return jax.shard_map(
        functools.partial(local, mesh.shape["loop"], mesh.shape["team"]),
        mesh=mesh,
        in_specs=(P(spec, None, None), P(spec, None), P(spec), P(spec)),
        out_specs=P(spec, None),
        check_vma=False,
    )
```

```python
import functools

import jax
import jax.numpy as jnp
from jax import lax
from jax.experimental import pallas as pl
from jax.experimental.pallas import tpu as pltpu
from jax.sharding import PartitionSpec as P

STOPS = 4
LANES = 128


def div(x, n):
    return lax.shift_right_logical(x, n.bit_length() - 1) if n & (n - 1) == 0 else lax.div(x, n)


def rem(x, n):
    return x & (n - 1) if n & (n - 1) == 0 else lax.rem(x, n)


def kernel(geo, col_ref, cnt_ref, blocks_ref, probes_ref, out_ref,
           blk, win, col_v, cnt_v, inv_v, inv_s, recv, send, loc):
    loop_n, team_n, chunks, rows_here, slots, edge, tps = geo
    chunk = tps * edge // chunks
    per_chunk = tps // chunks
    per_piece = team_n * tps
    span = STOPS * per_piece
    mates = range(1, team_n)
    t = lax.axis_index("loop")
    m = lax.axis_index("team")
    core = lax.rem(t, 2)
    lower = core == 0
    upper = core == 1
    odd = lax.rem(lax.div(t, 2), 2) == 1
    even = ~odd
    wrap_in = t < 4
    wrap_out = t >= loop_n - 2

    def at(dt, dm):
        return {"loop": lax.rem(t + dt + loop_n, loop_n), "team": lax.rem(m + dm + team_n, team_n)}

    own_copy = pltpu.make_async_copy(probes_ref, win.at[0, 0], loc.at[0])
    col_copy = pltpu.make_async_copy(col_ref, col_v.at[0], loc.at[1])
    cnt_copy = pltpu.make_async_copy(cnt_ref, cnt_v.at[0], loc.at[2])
    blk_copy = pltpu.make_async_copy(blocks_ref, blk.at[pl.ds(0, slots)], loc.at[3])
    own_copy.start()

    barrier = pltpu.get_barrier_semaphore()

    def greet(dt, dm):
        pl.semaphore_signal(barrier, inc=1, device_id=at(dt, dm), device_id_type=pl.DeviceIdType.MESH)

    greet(-3, 0)

    @pl.when(upper)
    def _():
        greet(-2, 0)
        for d in mates:
            greet(-1, d)
            greet(0, d)

    @pl.when(lower & odd)
    def _():
        pl.when(wrap_in)(lambda: greet(-1, 0))
        for d in mates:
            pl.when(~wrap_in)(lambda: greet(0, d))
    greet(1 - 2 * core, 0)

    for copy in (col_copy, cnt_copy, blk_copy):
        copy.start()

    near_odd = (odd & ~wrap_in).astype(jnp.int32)
    far_even = (even & wrap_in).astype(jnp.int32)
    pl.semaphore_wait(barrier, jnp.where(
        lower, team_n + 1 + (team_n - 1) * near_odd, team_n + 2 + far_even))

    own_copy.wait()

    groups = []

    def rows(c):
        return pl.ds(c * chunk if isinstance(c, int) else pl.multiple_of(c * chunk, chunk), chunk)

    def group(only=None, size=chunks):
        groups.append((only, size))
        return len(groups) - 1

    def push(g, src, k, d, c, where, always=False):
        copy = pltpu.make_async_remote_copy(
            src_ref=src, dst_ref=win.at[k, d, rows(c)],
            send_sem=send.at[g], recv_sem=recv.at[k, d, c],
            device_id=where, device_id_type=pl.DeviceIdType.MESH)
        if always or groups[g][0] is None:
            copy.start()
        else:
            pl.when(groups[g][0])(copy.start)

    def finish(g):
        only, size = groups[g]

        def wait():
            ref = win.at[0, 0, pl.ds(0, size * chunk)]
            pltpu.make_async_copy(ref, ref, send.at[g]).wait()
        if only is None:
            wait()
        else:
            pl.when(only)(wait)

    def arrive(k, d, c):
        ref = win.at[k, d, rows(c)]
        pltpu.make_async_copy(ref, ref, recv.at[k, d, c]).wait()
        return ref

    backward = range(chunks - 1, -1, -1)
    g_ahead = group()
    g_mate = {d: group() for d in mates}
    g_third = group(lower | ~(odd & wrap_out))

    def own(c):
        return win.at[0, 0, rows(c)]

    @pl.when(lower)
    def _():
        for c in range(chunks):
            for d in mates:
                push(g_mate[d], own(chunks - 1 - c), 1, d, chunks - 1 - c, at(1, d))
            push(g_ahead, own(c), 3, 0, c, at(3, 0))
        for c in range(chunks):
            push(g_third, own(c), 1, 0, c, at(1, 0), True)

    @pl.when(upper)
    def _():
        for c in range(chunks):
            for d in mates:
                push(g_mate[d], own(chunks - 1 - c), 0, d, chunks - 1 - c, at(0, d))
            push(g_ahead, own(c), 2, 0, c, at(2, 0))
        for c in range(chunks):
            push(g_third, own(c), 3, 0, c, at(3, 0))

    col_copy.wait()
    cnt_copy.wait()
    col = col_v[...]
    within = rem(col, per_piece)
    stop = rem(t - div(col, per_piece) + loop_n, loop_n)
    member = rem(m - div(within, tps) + team_n, team_n)
    key = (stop * team_n + member) * tps + rem(within, tps)
    number = lax.broadcasted_iota(jnp.int32, key.shape, 1)
    end = jnp.zeros((1, 1), jnp.int32)
    for r in range(rows_here):
        end = end + cnt_v[:, r:r + 1]
        key = key + jnp.where(number >= end, span, 0)
    key = jnp.where(number < end, key, -1)
    entries = inv_v.shape[1]
    keys = jnp.broadcast_to(key, (LANES, slots)).T[:, :1]
    hit = keys == lax.broadcasted_iota(jnp.int32, (slots, entries), 1)
    owner = jnp.where(hit, lax.broadcasted_iota(jnp.int32, (slots, entries), 0), slots)
    inv_v[...] = jnp.min(owner, axis=0, keepdims=True)
    inv_copy = pltpu.make_async_copy(inv_v, inv_s, loc.at[4])
    inv_copy.start()
    blk[slots] = jnp.zeros(blk.shape[1:], blk.dtype)
    inv_copy.wait()
    blk_copy.wait()

    def product(k, d, c, n):
        total = None
        step = 2 if (n * per_chunk) % 2 == 0 else 1
        for j in range(0, n * per_chunk, step):
            near = c * per_chunk + j
            base = (k * team_n + d) * tps + near
            left = []
            for r in range(rows_here):
                pair = [blk[inv_s[0, r * span + base + i]] for i in range(step)]
                left.append(jnp.concatenate(pair, axis=1))
            start = near * edge if isinstance(near, int) else pl.multiple_of(near * edge, edge)
            part = jnp.dot(jnp.concatenate(left, axis=0), win[k, d, pl.ds(start, step * edge)],
                           preferred_element_type=jnp.float32)
            total = part if total is None else total + part
        return total

    def compute(*parts, n=1):
        total = None
        for k, d, c in parts:
            part = product(k, d, c, n)
            total = part if total is None else total + part
        out_ref[...] += total

    def whole(*parts):
        compute(*((k, d, 0) for k, d in parts), n=chunks)

    out_ref[...] = product(0, 0, 0, chunks)

    def relayed(c):
        return c >= chunks // 4, c >= chunks - max(1, chunks // 2)

    def either(on_even, on_odd):
        if on_even == on_odd:
            return None if on_even else False
        return even if on_even else odd

    def upper_core():
        g_low_mate = {d: group() for d in mates}
        g_low_piece = {k: group() for k in (2, 3)}
        g_low_far = {(k, d): group() for k in (2, 3) for d in mates}
        g_third_mate = {d: group(even | wrap_out) for d in mates}
        g_side = group(even & wrap_in)
        g_on = {(k, d, c): group(either(*relayed(c)), 1) for k in (2, 3) for d in mates for c in range(chunks)
                if either(*relayed(c)) is not False}
        g_over = {(k, d, c): group(either(*(not x for x in relayed(c)[::-1])), 1)
                  for k in (2, 3) for d in mates for c in range(chunks)
                  if either(*(not x for x in relayed(c)[::-1])) is not False}
        late = odd & wrap_out

        def mate(c):
            for d in mates:
                got = arrive(0, d, c)
                if (2, d, c) in g_on:
                    push(g_on[2, d, c], got, 2, d, c, at(2, 0))
                pl.when(even)(lambda: push(g_third_mate[d], got, 3, d, c, at(3, 0), True))
                got = arrive(1, d, c)
                if (3, d, c) in g_on:
                    push(g_on[3, d, c], got, 3, d, c, at(2, 0))
                push(g_low_mate[d], got, 0, d, c, at(-1, 0))

        def piece(k, c):
            got = arrive(k, 0, c)
            for d in mates:
                if (k, d, c) in g_over:
                    push(g_over[k, d, c], got, k, d, c, at(0, d))
            push(g_low_piece[k], got, k - 1, 0, c, at(-1, 0))
            if k == 2:
                push(g_side, got, 3, 0, c, at(1, 0))

        def far(k, d, c):
            got = arrive(k, d, c)
            push(g_low_far[k, d], got, k - 1, d, c, at(-1, 0))

        for c in range(chunks):
            arrive(1, 0, c)
        whole((1, 0))
        for c in backward:
            mate(c)
        for d in mates:
            @pl.when(late)
            def _():
                if d == 1:
                    finish(g_ahead)
                for c in backward:
                    push(g_third_mate[d], win.at[0, d, rows(c)], 3, d, c, at(3, 0), True)
            whole((0, d), (1, d))

        @pl.when(~(even & wrap_in))
        def _():
            for c in range(chunks):
                for k in (3, 2):
                    piece(k, c)
                compute((3, 0, c), (2, 0, c))
            for i in range(chunks):
                c = 0 if i == 0 else jnp.where(odd, chunks - i, i)
                for d in mates:
                    for k in (3, 2):
                        far(k, d, c)
                    compute((3, d, c), (2, d, c))

        @pl.when(even & wrap_in)
        def _():
            for s in range(chunks + 2):
                if s < chunks:
                    for k in (3, 2):
                        piece(k, s)
                    compute((3, 0, s), (2, 0, s))
                if s >= 2:
                    for d in mates:
                        for k in (3, 2):
                            far(k, d, s - 2)
                        compute((3, d, s - 2), (2, d, s - 2))

    def lower_core():
        g_three = {d: group(odd & ~wrap_in) for d in mates}

        def mate():
            for d in mates:
                for c in backward:
                    arrive(0, d, c)
                whole((0, d))

        def third(forward):
            for c in range(chunks):
                got = arrive(3, 0, c)
                if forward:
                    for d in mates:
                        push(g_three[d], got, 3, d, c, at(0, d))
            whole((3, 0))

        def third_mate():
            for d in mates:
                for c in backward:
                    arrive(3, d, c)
                    compute((3, d, c))

        def pieces():
            for c in range(chunks):
                for k in (2, 1):
                    arrive(k, 0, c)
                compute((2, 0, c), (1, 0, c))

        def fars():
            for i in range(chunks):
                c = 0 if i == 0 else jnp.where(odd, chunks - i, i)
                for d in mates:
                    for k in (2, 1):
                        arrive(k, d, c)
                    compute((2, d, c), (1, d, c))

        mate()

        @pl.when(~wrap_in & even)
        def _():
            third(False)
            pieces()
            third_mate()
            fars()

        @pl.when(~wrap_in & odd)
        def _():
            third(True)
            pieces()
            fars()
            third_mate()

        @pl.when(wrap_in & odd)
        def _():
            pieces()
            fars()
            third(False)
            third_mate()

        @pl.when(wrap_in & even)
        def _():
            for s in range(chunks + 2):
                if s < chunks:
                    for k in (3, 2, 1):
                        arrive(k, 0, s)
                    compute((3, 0, s), (2, 0, s), (1, 0, s))
                for d in mates:
                    if 1 <= s <= chunks:
                        arrive(3, d, chunks - s)
                        compute((3, d, chunks - s))
                    if s >= 2:
                        for k in (2, 1):
                            arrive(k, d, s - 2)
                        compute((2, d, s - 2), (1, d, s - 2))

    def role(body):
        mark = len(groups)
        body()
        for g in range(mark, len(groups)):
            finish(g)
        del groups[mark:]

    pl.when(upper)(lambda: role(upper_core))
    pl.when(lower)(lambda: role(lower_core))

    @pl.when(lower | ~(odd & wrap_out))
    def _():
        finish(g_ahead)
    for d in mates:
        finish(g_mate[d])
    finish(g_third)


def sends(team_n, chunks):
    mates = team_n - 1
    return 5 + mates * (5 + 4 * chunks)


def in_hbm(x):
    return pltpu.with_memory_space_constraint(x, pltpu.HBM)


def local(loop_n, team_n, blocks, probes, row_count, column_of_slot):
    slots, edge, _ = blocks.shape
    width = probes.shape[1]
    tps = probes.shape[0] // edge
    rows_here = row_count.shape[0]
    chunks = min(4, tps)
    geo = (loop_n, team_n, chunks, rows_here, slots, edge, tps)
    entries = rows_here * STOPS * team_n * tps
    table = (1, -(-entries // LANES) * LANES)
    return pl.pallas_call(
        functools.partial(kernel, geo),
        out_shape=jax.ShapeDtypeStruct((rows_here * edge, width), jnp.float32),
        in_specs=[pl.BlockSpec(memory_space=pltpu.HBM)] * 4,
        out_specs=pl.BlockSpec(memory_space=pltpu.VMEM),
        scratch_shapes=[
            pltpu.VMEM((slots + 1, edge, edge), blocks.dtype),
            pltpu.VMEM((STOPS, team_n, tps * edge, width), probes.dtype),
            pltpu.VMEM((1, slots), jnp.int32),
            pltpu.VMEM((1, rows_here), jnp.int32),
            pltpu.VMEM(table, jnp.int32),
            pltpu.SMEM(table, jnp.int32),
            pltpu.SemaphoreType.DMA((STOPS, team_n, chunks)),
            pltpu.SemaphoreType.DMA((sends(team_n, chunks),)),
            pltpu.SemaphoreType.DMA((5,)),
        ],
        compiler_params=pltpu.CompilerParams(
            collective_id=0, has_side_effects=True, vmem_limit_bytes=55000 * 1024),
    )(in_hbm(column_of_slot), in_hbm(row_count), blocks, probes)


def solution(mesh):
    spec = ("loop", "team")
    return jax.shard_map(
        functools.partial(local, mesh.shape["loop"], mesh.shape["team"]),
        mesh=mesh,
        in_specs=(P(spec, None, None), P(spec, None), P(spec), P(spec)),
        out_specs=P(spec, None),
        check_vma=False,
    )
```

```python
import functools

import jax
import jax.numpy as jnp
from jax import lax
from jax.experimental import pallas as pl
from jax.experimental.pallas import tpu as pltpu
from jax.sharding import PartitionSpec as P

STOPS = 4
LANES = 128


def div(x, n):
    return lax.shift_right_logical(x, n.bit_length() - 1) if n & (n - 1) == 0 else lax.div(x, n)


def rem(x, n):
    return x & (n - 1) if n & (n - 1) == 0 else lax.rem(x, n)


def kernel(geo, col_ref, cnt_ref, blocks_ref, probes_ref, out_ref,
           blk, win, hop, col_v, cnt_v, inv_v, inv_s, recv, hop_recv, send, loc):
    loop_n, team_n, chunks, rows_here, slots, edge, tps = geo
    chunk = tps * edge // chunks
    per_chunk = tps // chunks
    per_piece = team_n * tps
    span = STOPS * per_piece
    mates = range(1, team_n)
    t = lax.axis_index("loop")
    m = lax.axis_index("team")
    core = lax.rem(t, 2)
    lower = core == 0
    upper = core == 1
    odd = lax.rem(lax.div(t, 2), 2) == 1
    even = ~odd
    wrap_in = t < 4
    wrap_out = t >= loop_n - 2
    hop_here = t == loop_n - 3
    hop_to = t == 1
    side = max(1, 1 * chunks // 4)

    def at(dt, dm):
        return {"loop": lax.rem(t + dt + loop_n, loop_n), "team": lax.rem(m + dm + team_n, team_n)}

    own_copy = pltpu.make_async_copy(probes_ref, win.at[0, 0], loc.at[0])
    col_copy = pltpu.make_async_copy(col_ref, col_v.at[0], loc.at[1])
    cnt_copy = pltpu.make_async_copy(cnt_ref, cnt_v.at[0], loc.at[2])
    blk_copy = pltpu.make_async_copy(blocks_ref, blk.at[pl.ds(0, slots)], loc.at[3])
    own_copy.start()

    barrier = pltpu.get_barrier_semaphore()

    def greet(dt, dm):
        pl.semaphore_signal(barrier, inc=1, device_id=at(dt, dm), device_id_type=pl.DeviceIdType.MESH)

    greet(-3, 0)

    @pl.when(upper)
    def _():
        greet(-2, 0)
        pl.when(even & ~wrap_in)(lambda: greet(1, 0))
        pl.when(hop_here)(lambda: greet(2, 0))
        pl.when(hop_to)(lambda: greet(-4, 0))
        for d in mates:
            greet(-1, d)
            greet(0, d)

    @pl.when(lower & odd)
    def _():
        pl.when(wrap_in)(lambda: greet(-1, 0))
        for d in mates:
            pl.when(~wrap_in)(lambda: greet(0, d))
    greet(1 - 2 * core, 0)

    col_copy.start()
    cnt_copy.start()

    near_odd = (odd & ~wrap_in).astype(jnp.int32)
    far_even = (even & wrap_in).astype(jnp.int32)
    pl.semaphore_wait(barrier, jnp.where(
        lower, team_n + 1 + team_n * near_odd,
        team_n + 2 + far_even + (hop_here | wrap_out).astype(jnp.int32)))

    own_copy.wait()

    groups = []

    def rows(c):
        return pl.ds(c * chunk if isinstance(c, int) else pl.multiple_of(c * chunk, chunk), chunk)

    def group(only=None, size=chunks):
        groups.append((only, size))
        return len(groups) - 1

    def push(g, src, k, d, c, where, always=False):
        copy = pltpu.make_async_remote_copy(
            src_ref=src, dst_ref=win.at[k, d, rows(c)],
            send_sem=send.at[g], recv_sem=recv.at[k, d, c],
            device_id=where, device_id_type=pl.DeviceIdType.MESH)
        if always or groups[g][0] is None:
            copy.start()
        else:
            pl.when(groups[g][0])(copy.start)

    def push_hop(g, src, slot, where):
        pltpu.make_async_remote_copy(
            src_ref=src, dst_ref=hop.at[slot], send_sem=send.at[g], recv_sem=hop_recv.at[slot],
            device_id=where, device_id_type=pl.DeviceIdType.MESH).start()

    def finish(g):
        only, size = groups[g]

        def wait():
            ref = win.at[0, 0, pl.ds(0, size * chunk)]
            pltpu.make_async_copy(ref, ref, send.at[g]).wait()
        if only is None:
            wait()
        else:
            pl.when(only)(wait)

    def arrive(k, d, c):
        ref = win.at[k, d, rows(c)]
        pltpu.make_async_copy(ref, ref, recv.at[k, d, c]).wait()
        return ref

    backward = range(chunks - 1, -1, -1)
    passed = lower | even | wrap_out
    g_ahead = group(passed)
    g_mate = {d: group() for d in mates}
    g_third = group(lower | ~(odd & wrap_out))

    def own(c):
        return win.at[0, 0, rows(c)]

    @pl.when(lower)
    def _():
        for c in range(chunks):
            for d in mates:
                push(g_mate[d], own(chunks - 1 - c), 1, d, chunks - 1 - c, at(1, d))
            if c < chunks - side:
                push(g_ahead, own(c), 3, 0, c, at(3, 0))
            else:
                pl.when(~(odd & wrap_out))(lambda: push(g_ahead, own(c), 3, 0, c, at(3, 0), True))
                pl.when(odd & wrap_out)(lambda: push_hop(g_ahead, own(c), c - chunks + side, at(-1, 0)))
        for c in range(chunks):
            push(g_third, own(c), 1, 0, c, at(1, 0), True)

    @pl.when(upper)
    def _():
        for c in range(chunks):
            for d in mates:
                push(g_mate[d], own(chunks - 1 - c), 0, d, chunks - 1 - c, at(0, d))
            if c < chunks - side:
                push(g_ahead, own(c), 2, 0, c, at(2, 0))
            else:
                pl.when(even)(lambda: push(g_ahead, own(c), 2, 0, c, at(2, 0), True))
                pl.when(wrap_out)(lambda: push_hop(g_ahead, own(c), c - chunks + 2 * side, at(-2, 0)))
            pl.when(odd)(lambda: push(g_third, own(c), 3, 0, c, at(3, 0)))
        for c in range(chunks):
            pl.when(even)(lambda: push(g_third, own(c), 3, 0, c, at(3, 0), True))

    blk_copy.start()
    col_copy.wait()
    cnt_copy.wait()
    col = col_v[...]
    within = rem(col, per_piece)
    stop = rem(t - div(col, per_piece) + loop_n, loop_n)
    member = rem(m - div(within, tps) + team_n, team_n)
    key = (stop * team_n + member) * tps + rem(within, tps)
    number = lax.broadcasted_iota(jnp.int32, key.shape, 1)
    end = jnp.zeros((1, 1), jnp.int32)
    for r in range(rows_here):
        end = end + cnt_v[:, r:r + 1]
        key = key + jnp.where(number >= end, span, 0)
    key = jnp.where(number < end, key, -1)
    entries = inv_v.shape[1]
    keys = jnp.broadcast_to(key, (LANES, slots)).T[:, :1]
    hit = keys == lax.broadcasted_iota(jnp.int32, (slots, entries), 1)
    owner = jnp.where(hit, lax.broadcasted_iota(jnp.int32, (slots, entries), 0), slots)
    inv_v[...] = jnp.min(owner, axis=0, keepdims=True)
    inv_copy = pltpu.make_async_copy(inv_v, inv_s, loc.at[4])
    inv_copy.start()
    blk[slots] = jnp.zeros(blk.shape[1:], blk.dtype)
    inv_copy.wait()
    blk_copy.wait()

    def product(k, d, c, n):
        total = None
        step = 2 if (n * per_chunk) % 2 == 0 else 1
        for j in range(0, n * per_chunk, step):
            near = c * per_chunk + j
            base = (k * team_n + d) * tps + near
            left = []
            for r in range(rows_here):
                pair = [blk[inv_s[0, r * span + base + i]] for i in range(step)]
                left.append(jnp.concatenate(pair, axis=1))
            start = near * edge if isinstance(near, int) else pl.multiple_of(near * edge, edge)
            part = jnp.dot(jnp.concatenate(left, axis=0), win[k, d, pl.ds(start, step * edge)],
                           preferred_element_type=jnp.float32)
            total = part if total is None else total + part
        return total

    def compute(*parts, n=1):
        total = None
        for k, d, c in parts:
            part = product(k, d, c, n)
            total = part if total is None else total + part
        out_ref[...] += total

    def whole(*parts):
        compute(*((k, d, 0) for k, d in parts), n=chunks)

    out_ref[...] = product(0, 0, 0, chunks)

    def relayed(k, c):
        return c >= chunks // 4, k == 2, c >= chunks - (2 if k == 2 else 2) * chunks // 4

    def where(flags, is_far, swap):
        masks = (odd, even & ~is_far, even & is_far) if swap else (even, odd & ~is_far, odd & is_far)
        chosen = [mask for mask, flag in zip(masks, flags) if flag]
        if len(chosen) in (0, 3):
            return None if chosen else False
        return functools.reduce(jnp.logical_or, chosen)

    halves = [range(0, (chunks + 1) // 2), range((chunks + 1) // 2, chunks)]
    ends = {run[-1]: run for run in halves if len(run)}

    def upper_core():
        g_low_mate = {d: group() for d in mates}
        g_low_piece = {k: group() for k in (2, 3)}
        g_low_far = {(k, d): group() for k in (2, 3) for d in mates}
        g_third_mate = {d: group(even | wrap_out) for d in mates}
        g_side = group(even & wrap_in)
        g_on, g_over = {}, {}
        for k in (2, 3):
            for c in range(chunks):
                flags = relayed(k, c)
                on = where(flags, wrap_out, False)
                over = where([not flag for flag in flags], wrap_in, True)
                for d in mates:
                    if on is not False:
                        g_on[k, d, c] = group(on, 1)
                    if over is not False:
                        g_over[k, d, c] = group(over, 1)
        late = odd & wrap_out

        def mate(c):
            for d in mates:
                got = arrive(0, d, c)
                if (2, d, c) in g_on:
                    push(g_on[2, d, c], got, 2, d, c, at(2, 0))
                pl.when(even)(lambda: push(g_third_mate[d], got, 3, d, c, at(3, 0), True))
                got = arrive(1, d, c)
                if (3, d, c) in g_on:
                    push(g_on[3, d, c], got, 3, d, c, at(2, 0))
                push(g_low_mate[d], got, 0, d, c, at(-1, 0))

        def piece(k, c):
            got = arrive(k, 0, c)
            for d in mates:
                if (k, d, c) in g_over:
                    push(g_over[k, d, c], got, k, d, c, at(0, d))
            push(g_low_piece[k], got, k - 1, 0, c, at(-1, 0))
            if k == 2:
                push(g_side, got, 3, 0, c, at(1, 0))

        def far(k, d, c):
            got = arrive(k, d, c)
            push(g_low_far[k, d], got, k - 1, d, c, at(-1, 0))

        g_hop = group(hop_here, 2 * side)
        for i, c in enumerate(backward):
            mate(c)
            if i < side:
                @pl.when(hop_here)
                def _():
                    for k in (2, 3):
                        slot = i + (3 - k) * side
                        pltpu.make_async_copy(hop.at[slot], hop.at[slot], hop_recv.at[slot]).wait()
                        push(g_hop, hop.at[slot], k, 0, chunks - side + i, at(4, 0), True)
        for d in mates:
            @pl.when(late)
            def _():
                if d == 1:
                    finish(g_ahead)
                for c in backward:
                    push(g_third_mate[d], win.at[0, d, rows(c)], 3, d, c, at(3, 0), True)

        def early():
            for c in range(chunks):
                arrive(1, 0, c)
            whole((1, 0), *((k, d) for d in mates for k in (0, 1)))

        @pl.when(~(even & wrap_in))
        def _():
            for c in range(chunks):
                piece(3, c)

            @pl.when(odd)
            def _():
                for c in range(chunks):
                    piece(2, c)
            early()

            @pl.when(even)
            def _():
                for c in range(chunks):
                    piece(2, c)
            whole((3, 0), (2, 0))
            for run in halves:
                parts = []
                for i in run:
                    c3 = 0 if i == 0 else jnp.where(odd, chunks - i, i)
                    c2 = jnp.where(odd, 0 if i == 0 else chunks - i, chunks - 1 - i)
                    for d in mates:
                        far(3, d, c3)
                        far(2, d, c2)
                        parts += [(3, d, c3), (2, d, c2)]
                compute(*parts)

        @pl.when(even & wrap_in)
        def _():
            for s in range(chunks + 2):
                if s < chunks:
                    for k in (2, 3):
                        piece(k, s)
                if s >= 2:
                    for d in mates:
                        for k in (2, 3):
                            far(k, d, s - 2)
            for c in range(chunks):
                arrive(1, 0, c)
            whole((1, 0), (3, 0), (2, 0), *((k, d) for d in mates for k in range(4)))

    def lower_core():
        g_three = {d: group(odd & ~wrap_in) for d in mates}
        g_back = group(odd & ~wrap_in)

        def mate():
            for d in mates:
                for c in backward:
                    arrive(0, d, c)
                whole((0, d))

        def third(forward):
            for c in range(chunks):
                got = arrive(3, 0, c)
                if forward:
                    push(g_back, got, 2, 0, c, at(-1, 0))
                    for d in mates:
                        push(g_three[d], got, 3, d, c, at(0, d))
            whole((3, 0))

        def third_mate():
            for d in mates:
                for run in halves:
                    for i in run:
                        arrive(3, d, chunks - 1 - i)
                    compute(*((3, d, chunks - 1 - i) for i in run))

        def pieces():
            for c in range(chunks):
                for k in (2, 1):
                    arrive(k, 0, c)
            whole((2, 0), (1, 0))

        def fars():
            for run in halves:
                parts = []
                for i in run:
                    c2 = 0 if i == 0 else jnp.where(odd, chunks - i, i)
                    c1 = jnp.where(odd, 0 if i == 0 else chunks - i, chunks - 1 - i)
                    for d in mates:
                        arrive(2, d, c2)
                        arrive(1, d, c1)
                        parts += [(2, d, c2), (1, d, c1)]
                compute(*parts)

        @pl.when(~wrap_in & even)
        def _():
            mate()
            third(False)
            pieces()
            third_mate()
            fars()

        @pl.when(~wrap_in & odd)
        def _():
            third(True)
            mate()
            pieces()
            fars()
            third_mate()

        @pl.when(wrap_in & odd)
        def _():
            mate()
            pieces()
            fars()
            third(False)
            third_mate()

        @pl.when(wrap_in & even)
        def _():
            mate()
            for c in range(chunks):
                for k in (3, 1, 2):
                    arrive(k, 0, c)
                compute(*((k, 0, c) for k in (3, 2, 1)))
            for run in halves:
                for d in mates:
                    for c in run:
                        arrive(3, d, chunks - 1 - c)
                    compute(*((3, d, chunks - 1 - c) for c in run))
                for d in mates:
                    for c in run:
                        for k in (1, 2):
                            arrive(k, d, c)
                    compute(*((k, d, c) for k in (2, 1) for c in run))

    def role(body):
        mark = len(groups)
        body()
        for g in range(mark, len(groups)):
            finish(g)
        del groups[mark:]

    pl.when(upper)(lambda: role(upper_core))
    pl.when(lower)(lambda: role(lower_core))

    @pl.when(lower | even)
    def _():
        finish(g_ahead)
    for d in mates:
        finish(g_mate[d])
    finish(g_third)


def sends(team_n, chunks):
    mates = team_n - 1
    return 6 + mates * (5 + 4 * chunks)


def in_hbm(x):
    return pltpu.with_memory_space_constraint(x, pltpu.HBM)


def local(loop_n, team_n, blocks, probes, row_count, column_of_slot):
    slots, edge, _ = blocks.shape
    width = probes.shape[1]
    tps = probes.shape[0] // edge
    rows_here = row_count.shape[0]
    chunks = min(4, tps)
    hops = max(1, 1 * chunks // 4)
    geo = (loop_n, team_n, chunks, rows_here, slots, edge, tps)
    entries = rows_here * STOPS * team_n * tps
    table = (1, -(-entries // LANES) * LANES)
    return pl.pallas_call(
        functools.partial(kernel, geo),
        out_shape=jax.ShapeDtypeStruct((rows_here * edge, width), jnp.float32),
        in_specs=[pl.BlockSpec(memory_space=pltpu.HBM)] * 4,
        out_specs=pl.BlockSpec(memory_space=pltpu.VMEM),
        scratch_shapes=[
            pltpu.VMEM((slots + 1, edge, edge), blocks.dtype),
            pltpu.VMEM((STOPS, team_n, tps * edge, width), probes.dtype),
            pltpu.VMEM((2 * hops, tps * edge // chunks, width), probes.dtype),
            pltpu.VMEM((1, slots), jnp.int32),
            pltpu.VMEM((1, rows_here), jnp.int32),
            pltpu.VMEM(table, jnp.int32),
            pltpu.SMEM(table, jnp.int32),
            pltpu.SemaphoreType.DMA((STOPS, team_n, chunks)),
            pltpu.SemaphoreType.DMA((2 * hops,)),
            pltpu.SemaphoreType.DMA((sends(team_n, chunks),)),
            pltpu.SemaphoreType.DMA((5,)),
        ],
        compiler_params=pltpu.CompilerParams(
            collective_id=0, has_side_effects=True, vmem_limit_bytes=55000 * 1024),
    )(in_hbm(column_of_slot), in_hbm(row_count), blocks, probes)


def solution(mesh):
    spec = ("loop", "team")
    return jax.shard_map(
        functools.partial(local, mesh.shape["loop"], mesh.shape["team"]),
        mesh=mesh,
        in_specs=(P(spec, None, None), P(spec, None), P(spec), P(spec)),
        out_specs=P(spec, None),
        check_vma=False,
    )
```

```python
import functools

import jax
import jax.numpy as jnp
from jax import lax
from jax.experimental import pallas as pl
from jax.experimental.pallas import tpu as pltpu
from jax.sharding import PartitionSpec as P

STOPS = 4
LANES = 128


def div(x, n):
    return lax.shift_right_logical(x, n.bit_length() - 1) if n & (n - 1) == 0 else lax.div(x, n)


def rem(x, n):
    return x & (n - 1) if n & (n - 1) == 0 else lax.rem(x, n)


def kernel(geo, col_ref, cnt_ref, blocks_ref, probes_ref, out_ref,
           blk, win, hop, col_v, cnt_v, inv_v, inv_s, recv, hop_recv, send, loc):
    loop_n, team_n, chunks, rows_here, slots, edge, tps = geo
    chunk = tps * edge // chunks
    per_chunk = tps // chunks
    per_piece = team_n * tps
    span = STOPS * per_piece
    mates = range(1, team_n)
    t = lax.axis_index("loop")
    m = lax.axis_index("team")
    core = lax.rem(t, 2)
    lower = core == 0
    upper = core == 1
    odd = lax.rem(lax.div(t, 2), 2) == 1
    even = ~odd
    wrap_in = t < 4
    wrap_out = t >= loop_n - 2
    hop_here = t == loop_n - 3
    hop_to = t == 1
    side = max(1, chunks // 4)

    def at(dt, dm):
        return {"loop": lax.rem(t + dt + loop_n, loop_n), "team": lax.rem(m + dm + team_n, team_n)}

    own_copy = pltpu.make_async_copy(probes_ref, win.at[0, 0], loc.at[0])
    col_copy = pltpu.make_async_copy(col_ref, col_v.at[0], loc.at[1])
    cnt_copy = pltpu.make_async_copy(cnt_ref, cnt_v.at[0], loc.at[2])
    blk_copy = pltpu.make_async_copy(blocks_ref, blk.at[pl.ds(0, slots)], loc.at[3])
    own_copy.start()

    barrier = pltpu.get_barrier_semaphore()

    def greet(dt, dm):
        pl.semaphore_signal(barrier, inc=1, device_id=at(dt, dm), device_id_type=pl.DeviceIdType.MESH)

    greet(-3, 0)

    @pl.when(upper)
    def _():
        greet(-2, 0)
        pl.when(even & ~wrap_in)(lambda: greet(1, 0))
        pl.when(hop_here)(lambda: greet(2, 0))
        pl.when(hop_to)(lambda: greet(-4, 0))
        for d in mates:
            greet(-1, d)
            greet(0, d)

    @pl.when(lower & odd)
    def _():
        pl.when(wrap_in)(lambda: greet(-1, 0))
        for d in mates:
            pl.when(~wrap_in)(lambda: greet(0, d))
    greet(1 - 2 * core, 0)

    col_copy.start()
    cnt_copy.start()

    near_odd = (odd & ~wrap_in).astype(jnp.int32)
    far_even = (even & wrap_in).astype(jnp.int32)
    pl.semaphore_wait(barrier, jnp.where(
        lower, team_n + 1 + team_n * near_odd,
        team_n + 2 + far_even + (hop_here | wrap_out).astype(jnp.int32)))

    own_copy.wait()

    groups = []

    def rows(c):
        return pl.ds(c * chunk if isinstance(c, int) else pl.multiple_of(c * chunk, chunk), chunk)

    def group(only=None, size=chunks):
        groups.append((only, size))
        return len(groups) - 1

    def push(g, src, k, d, c, where, always=False):
        copy = pltpu.make_async_remote_copy(
            src_ref=src, dst_ref=win.at[k, d, rows(c)],
            send_sem=send.at[g], recv_sem=recv.at[k, d, c],
            device_id=where, device_id_type=pl.DeviceIdType.MESH)
        if always or groups[g][0] is None:
            copy.start()
        else:
            pl.when(groups[g][0])(copy.start)

    def push_hop(g, src, slot, where):
        pltpu.make_async_remote_copy(
            src_ref=src, dst_ref=hop.at[slot], send_sem=send.at[g], recv_sem=hop_recv.at[slot],
            device_id=where, device_id_type=pl.DeviceIdType.MESH).start()

    def finish(g):
        only, size = groups[g]

        def wait():
            ref = win.at[0, 0, pl.ds(0, size * chunk)]
            pltpu.make_async_copy(ref, ref, send.at[g]).wait()
        if only is None:
            wait()
        else:
            pl.when(only)(wait)

    def arrive(k, d, c):
        ref = win.at[k, d, rows(c)]
        pltpu.make_async_copy(ref, ref, recv.at[k, d, c]).wait()
        return ref

    backward = range(chunks - 1, -1, -1)
    passed = lower | even | wrap_out
    g_ahead = group(passed)
    g_mate = {d: group() for d in mates}
    g_third = group(lower | ~(odd & wrap_out))

    def own(c):
        return win.at[0, 0, rows(c)]

    @pl.when(lower)
    def _():
        for c in range(chunks):
            for d in mates:
                push(g_mate[d], own(chunks - 1 - c), 1, d, chunks - 1 - c, at(1, d))
            if c < chunks - side:
                push(g_ahead, own(c), 3, 0, c, at(3, 0))
            else:
                pl.when(~(odd & wrap_out))(lambda: push(g_ahead, own(c), 3, 0, c, at(3, 0), True))
                pl.when(odd & wrap_out)(lambda: push_hop(g_ahead, own(c), c - chunks + side, at(-1, 0)))
        for c in range(chunks):
            push(g_third, own(c), 1, 0, c, at(1, 0), True)

    @pl.when(upper)
    def _():
        for c in range(chunks):
            for d in mates:
                push(g_mate[d], own(chunks - 1 - c), 0, d, chunks - 1 - c, at(0, d))
            if c < chunks - side:
                push(g_ahead, own(c), 2, 0, c, at(2, 0))
            else:
                pl.when(even)(lambda: push(g_ahead, own(c), 2, 0, c, at(2, 0), True))
                pl.when(wrap_out)(lambda: push_hop(g_ahead, own(c), c - chunks + 2 * side, at(-2, 0)))
            pl.when(odd)(lambda: push(g_third, own(c), 3, 0, c, at(3, 0)))
        for c in range(chunks):
            pl.when(even)(lambda: push(g_third, own(c), 3, 0, c, at(3, 0), True))

    blk_copy.start()
    col_copy.wait()
    cnt_copy.wait()
    col = col_v[...]
    within = rem(col, per_piece)
    stop = rem(t - div(col, per_piece) + loop_n, loop_n)
    member = rem(m - div(within, tps) + team_n, team_n)
    key = (stop * team_n + member) * tps + rem(within, tps)
    number = lax.broadcasted_iota(jnp.int32, key.shape, 1)
    end = jnp.zeros((1, 1), jnp.int32)
    for r in range(rows_here):
        end = end + cnt_v[:, r:r + 1]
        key = key + jnp.where(number >= end, span, 0)
    key = jnp.where(number < end, key, -1)
    entries = inv_v.shape[1]
    keys = jnp.broadcast_to(key, (LANES, slots)).T[:, :1]
    hit = keys == lax.broadcasted_iota(jnp.int32, (slots, entries), 1)
    owner = jnp.where(hit, lax.broadcasted_iota(jnp.int32, (slots, entries), 0), slots)
    inv_v[...] = jnp.min(owner, axis=0, keepdims=True)
    inv_copy = pltpu.make_async_copy(inv_v, inv_s, loc.at[4])
    inv_copy.start()
    blk[slots] = jnp.zeros(blk.shape[1:], blk.dtype)
    inv_copy.wait()
    blk_copy.wait()

    def product(k, d, c, n):
        total = None
        step = 2 if (n * per_chunk) % 2 == 0 else 1
        for j in range(0, n * per_chunk, step):
            near = c * per_chunk + j
            base = (k * team_n + d) * tps + near
            left = []
            for r in range(rows_here):
                pair = [blk[inv_s[0, r * span + base + i]] for i in range(step)]
                left.append(jnp.concatenate(pair, axis=1))
            start = near * edge if isinstance(near, int) else pl.multiple_of(near * edge, edge)
            part = jnp.dot(jnp.concatenate(left, axis=0), win[k, d, pl.ds(start, step * edge)],
                           preferred_element_type=jnp.float32)
            total = part if total is None else total + part
        return total

    def compute(*parts, n=1):
        total = None
        for k, d, c in parts:
            part = product(k, d, c, n)
            total = part if total is None else total + part
        out_ref[...] += total

    def whole(*parts):
        compute(*((k, d, 0) for k, d in parts), n=chunks)

    out_ref[...] = product(0, 0, 0, chunks)

    def relayed(k, c):
        return c >= chunks // 4, k == 2, c >= chunks - chunks // 2

    def where(flags, is_far, swap):
        masks = (odd, even & ~is_far, even & is_far) if swap else (even, odd & ~is_far, odd & is_far)
        chosen = [mask for mask, flag in zip(masks, flags) if flag]
        if len(chosen) in (0, 3):
            return None if chosen else False
        return functools.reduce(jnp.logical_or, chosen)

    halves = [range(0, (chunks + 1) // 2), range((chunks + 1) // 2, chunks)]
    ends = {run[-1]: run for run in halves if len(run)}

    def upper_core():
        g_low_mate = {d: group() for d in mates}
        g_low_piece = {k: group() for k in (2, 3)}
        g_low_far = {(k, d): group() for k in (2, 3) for d in mates}
        g_third_mate = {d: group(even | wrap_out) for d in mates}
        g_side = group(even & wrap_in)
        g_on, g_over = {}, {}
        for k in (2, 3):
            for c in range(chunks):
                flags = relayed(k, c)
                on = where(flags, wrap_out, False)
                over = where([not flag for flag in flags], wrap_in, True)
                for d in mates:
                    if on is not False:
                        g_on[k, d, c] = group(on, 1)
                    if over is not False:
                        g_over[k, d, c] = group(over, 1)
        late = odd & wrap_out

        def mate(c):
            for d in mates:
                got = arrive(0, d, c)
                if (2, d, c) in g_on:
                    push(g_on[2, d, c], got, 2, d, c, at(2, 0))
                pl.when(even)(lambda: push(g_third_mate[d], got, 3, d, c, at(3, 0), True))
                got = arrive(1, d, c)
                if (3, d, c) in g_on:
                    push(g_on[3, d, c], got, 3, d, c, at(2, 0))
                push(g_low_mate[d], got, 0, d, c, at(-1, 0))

        def piece(k, c):
            got = arrive(k, 0, c)
            for d in mates:
                if (k, d, c) in g_over:
                    push(g_over[k, d, c], got, k, d, c, at(0, d))
            push(g_low_piece[k], got, k - 1, 0, c, at(-1, 0))
            if k == 2:
                push(g_side, got, 3, 0, c, at(1, 0))

        def far(k, d, c):
            got = arrive(k, d, c)
            push(g_low_far[k, d], got, k - 1, d, c, at(-1, 0))

        g_hop = group(hop_here, 2 * side)
        for i, c in enumerate(backward):
            mate(c)
            if i < side:
                @pl.when(hop_here)
                def _():
                    for k in (2, 3):
                        slot = i + (3 - k) * side
                        pltpu.make_async_copy(hop.at[slot], hop.at[slot], hop_recv.at[slot]).wait()
                        push(g_hop, hop.at[slot], k, 0, chunks - side + i, at(4, 0), True)
        for d in mates:
            @pl.when(late)
            def _():
                if d == 1:
                    finish(g_ahead)
                for c in backward:
                    push(g_third_mate[d], win.at[0, d, rows(c)], 3, d, c, at(3, 0), True)

        def early():
            for c in range(chunks):
                arrive(1, 0, c)
            whole((1, 0), *((k, d) for d in mates for k in (0, 1)))

        @pl.when(~(even & wrap_in))
        def _():
            for c in range(chunks):
                piece(3, c)

            @pl.when(odd)
            def _():
                for c in range(chunks):
                    piece(2, c)
            early()

            @pl.when(even)
            def _():
                for c in range(chunks):
                    piece(2, c)
            whole((3, 0), (2, 0))
            for run in halves:
                parts = []
                for i in run:
                    c3 = 0 if i == 0 else jnp.where(odd, chunks - i, i)
                    c2 = jnp.where(odd, 0 if i == 0 else chunks - i, chunks - 1 - i)
                    for d in mates:
                        far(3, d, c3)
                        far(2, d, c2)
                        parts += [(3, d, c3), (2, d, c2)]
                compute(*parts)

        def back_at(i):
            return i if i < chunks - chunks // 2 else 2 * chunks - 1 - chunks // 2 - i

        @pl.when(even & wrap_in)
        def _():
            for s in range(chunks + 2):
                if s < chunks:
                    for k in (2, 3):
                        piece(k, s)
                if s >= 2:
                    for d in mates:
                        for k in (2, 3):
                            far(k, d, back_at(s - 2))
            for c in range(chunks):
                arrive(1, 0, c)
            whole((1, 0), (3, 0), (2, 0), *((k, d) for d in mates for k in range(4)))

    def lower_core():
        g_three = {d: group(odd & ~wrap_in) for d in mates}
        g_back = group(odd & ~wrap_in)

        def mate():
            for d in mates:
                for c in backward:
                    arrive(0, d, c)
                whole((0, d))

        def third(forward):
            for c in range(chunks):
                got = arrive(3, 0, c)
                if forward:
                    push(g_back, got, 2, 0, c, at(-1, 0))
                    for d in mates:
                        push(g_three[d], got, 3, d, c, at(0, d))
            whole((3, 0))

        def third_mate():
            for d in mates:
                for c in backward:
                    arrive(3, d, c)
                whole((3, d))

        def pieces():
            for c in range(chunks):
                for k in (2, 1):
                    arrive(k, 0, c)
            whole((2, 0), (1, 0))

        def fars():
            for run in halves:
                parts = []
                for i in run:
                    c2 = 0 if i == 0 else jnp.where(odd, chunks - i, i)
                    c1 = jnp.where(odd, 0 if i == 0 else chunks - i, chunks - 1 - i)
                    for d in mates:
                        arrive(2, d, c2)
                        arrive(1, d, c1)
                        parts += [(2, d, c2), (1, d, c1)]
                compute(*parts)

        @pl.when(~wrap_in & even)
        def _():
            mate()
            third(False)
            pieces()
            third_mate()
            fars()

        @pl.when(~wrap_in & odd)
        def _():
            third(True)
            mate()
            pieces()
            fars()
            third_mate()

        @pl.when(wrap_in & odd)
        def _():
            mate()
            pieces()
            fars()
            third(False)
            third_mate()

        @pl.when(wrap_in & even)
        def _():
            mate()
            for c in range(chunks):
                for k in (3, 1, 2):
                    arrive(k, 0, c)
            whole((3, 0), (2, 0), (1, 0))
            for run in halves:
                parts = []
                for d in mates:
                    for c in run:
                        parts += [(3, d, chunks - 1 - c), (1, d, c), (2, d, c)]
                for part in parts:
                    arrive(*part)
                compute(*parts)

    def role(body):
        mark = len(groups)
        body()
        for g in range(mark, len(groups)):
            finish(g)
        del groups[mark:]

    pl.when(upper)(lambda: role(upper_core))
    pl.when(lower)(lambda: role(lower_core))

    @pl.when(lower | even)
    def _():
        finish(g_ahead)
    for d in mates:
        finish(g_mate[d])
    finish(g_third)


def sends(team_n, chunks):
    mates = team_n - 1
    return 6 + mates * (5 + 4 * chunks)


def in_hbm(x):
    return pltpu.with_memory_space_constraint(x, pltpu.HBM)


def local(loop_n, team_n, blocks, probes, row_count, column_of_slot):
    slots, edge, _ = blocks.shape
    width = probes.shape[1]
    tps = probes.shape[0] // edge
    rows_here = row_count.shape[0]
    chunks = min(4, tps)
    hops = max(1, chunks // 4)
    geo = (loop_n, team_n, chunks, rows_here, slots, edge, tps)
    entries = rows_here * STOPS * team_n * tps
    table = (1, -(-entries // LANES) * LANES)
    return pl.pallas_call(
        functools.partial(kernel, geo),
        out_shape=jax.ShapeDtypeStruct((rows_here * edge, width), jnp.float32),
        in_specs=[pl.BlockSpec(memory_space=pltpu.HBM)] * 4,
        out_specs=pl.BlockSpec(memory_space=pltpu.VMEM),
        scratch_shapes=[
            pltpu.VMEM((slots + 1, edge, edge), blocks.dtype),
            pltpu.VMEM((STOPS, team_n, tps * edge, width), probes.dtype),
            pltpu.VMEM((2 * hops, tps * edge // chunks, width), probes.dtype),
            pltpu.VMEM((1, slots), jnp.int32),
            pltpu.VMEM((1, rows_here), jnp.int32),
            pltpu.VMEM(table, jnp.int32),
            pltpu.SMEM(table, jnp.int32),
            pltpu.SemaphoreType.DMA((STOPS, team_n, chunks)),
            pltpu.SemaphoreType.DMA((2 * hops,)),
            pltpu.SemaphoreType.DMA((sends(team_n, chunks),)),
            pltpu.SemaphoreType.DMA((5,)),
        ],
        compiler_params=pltpu.CompilerParams(
            collective_id=0, has_side_effects=True, vmem_limit_bytes=55000 * 1024),
    )(in_hbm(column_of_slot), in_hbm(row_count), blocks, probes)


def solution(mesh):
    spec = ("loop", "team")
    return jax.shard_map(
        functools.partial(local, mesh.shape["loop"], mesh.shape["team"]),
        mesh=mesh,
        in_specs=(P(spec, None, None), P(spec, None), P(spec), P(spec)),
        out_specs=P(spec, None),
        check_vma=False,
    )
```

```python
import functools

import jax
import jax.numpy as jnp
from jax import lax
from jax.experimental import pallas as pl
from jax.experimental.pallas import tpu as pltpu
from jax.sharding import PartitionSpec as P

STOPS = 4
LANES = 128


def div(x, n):
    return lax.shift_right_logical(x, n.bit_length() - 1) if n & (n - 1) == 0 else lax.div(x, n)


def rem(x, n):
    return x & (n - 1) if n & (n - 1) == 0 else lax.rem(x, n)


def kernel(geo, col_ref, cnt_ref, blocks_ref, probes_ref, out_ref,
           blk, win, hop, col_v, cnt_v, inv_v, inv_s, recv, hop_recv, send, loc):
    loop_n, team_n, chunks, rows_here, slots, edge, tps = geo
    chunk = tps * edge // chunks
    per_chunk = tps // chunks
    per_piece = team_n * tps
    span = STOPS * per_piece
    mates = range(1, team_n)
    t = lax.axis_index("loop")
    m = lax.axis_index("team")
    core = lax.rem(t, 2)
    lower = core == 0
    upper = core == 1
    odd = lax.rem(lax.div(t, 2), 2) == 1
    even = ~odd
    wrap_in = t < 4
    wrap_out = t >= loop_n - 2
    hop_here = t == loop_n - 3
    hop_to = t == 1
    side = max(1, chunks // 4)

    def at(dt, dm):
        return {"loop": lax.rem(t + dt + loop_n, loop_n), "team": lax.rem(m + dm + team_n, team_n)}

    own_copy = pltpu.make_async_copy(probes_ref, win.at[0, 0], loc.at[0])
    col_copy = pltpu.make_async_copy(col_ref, col_v.at[0], loc.at[1])
    cnt_copy = pltpu.make_async_copy(cnt_ref, cnt_v.at[0], loc.at[2])
    blk_copy = pltpu.make_async_copy(blocks_ref, blk.at[pl.ds(0, slots)], loc.at[3])
    own_copy.start()

    barrier = pltpu.get_barrier_semaphore()

    def greet(dt, dm):
        pl.semaphore_signal(barrier, inc=1, device_id=at(dt, dm), device_id_type=pl.DeviceIdType.MESH)

    greet(-3, 0)

    @pl.when(upper)
    def _():
        greet(-2, 0)
        pl.when(even & ~wrap_in)(lambda: greet(1, 0))
        pl.when(hop_here)(lambda: greet(2, 0))
        pl.when(hop_to)(lambda: greet(-4, 0))
        for d in mates:
            greet(-1, d)
            greet(0, d)

    @pl.when(lower & odd)
    def _():
        pl.when(wrap_in)(lambda: greet(-1, 0))
        for d in mates:
            pl.when(~wrap_in)(lambda: greet(0, d))
    greet(1 - 2 * core, 0)

    col_copy.start()
    cnt_copy.start()

    near_odd = (odd & ~wrap_in).astype(jnp.int32)
    far_even = (even & wrap_in).astype(jnp.int32)
    pl.semaphore_wait(barrier, jnp.where(
        lower, team_n + 1 + team_n * near_odd,
        team_n + 2 + far_even + (hop_here | wrap_out).astype(jnp.int32)))

    own_copy.wait()

    groups = []

    def rows(c):
        return pl.ds(c * chunk if isinstance(c, int) else pl.multiple_of(c * chunk, chunk), chunk)

    def group(only=None, size=chunks):
        groups.append((only, size))
        return len(groups) - 1

    def push(g, src, k, d, c, where, always=False):
        copy = pltpu.make_async_remote_copy(
            src_ref=src, dst_ref=win.at[k, d, rows(c)],
            send_sem=send.at[g], recv_sem=recv.at[k, d, c],
            device_id=where, device_id_type=pl.DeviceIdType.MESH)
        if always or groups[g][0] is None:
            copy.start()
        else:
            pl.when(groups[g][0])(copy.start)

    def push_hop(g, src, slot, where):
        pltpu.make_async_remote_copy(
            src_ref=src, dst_ref=hop.at[slot], send_sem=send.at[g], recv_sem=hop_recv.at[slot],
            device_id=where, device_id_type=pl.DeviceIdType.MESH).start()

    def finish(g):
        only, size = groups[g]

        def wait():
            ref = win.at[0, 0, pl.ds(0, size * chunk)]
            pltpu.make_async_copy(ref, ref, send.at[g]).wait()
        if only is None:
            wait()
        else:
            pl.when(only)(wait)

    def arrive(k, d, c):
        ref = win.at[k, d, rows(c)]
        pltpu.make_async_copy(ref, ref, recv.at[k, d, c]).wait()
        return ref

    backward = range(chunks - 1, -1, -1)
    passed = lower | even | wrap_out
    g_ahead = group(passed)
    g_mate = {d: group() for d in mates}
    g_third = group(lower | ~(odd & wrap_out))

    def own(c):
        return win.at[0, 0, rows(c)]

    @pl.when(lower)
    def _():
        for c in range(chunks):
            for d in mates:
                push(g_mate[d], own(chunks - 1 - c), 1, d, chunks - 1 - c, at(1, d))
            if c < chunks - side:
                push(g_ahead, own(c), 3, 0, c, at(3, 0))
            else:
                pl.when(~(odd & wrap_out))(lambda: push(g_ahead, own(c), 3, 0, c, at(3, 0), True))
                pl.when(odd & wrap_out)(lambda: push_hop(g_ahead, own(c), c - chunks + side, at(-1, 0)))
        for c in range(chunks):
            push(g_third, own(c), 1, 0, c, at(1, 0), True)

    @pl.when(upper)
    def _():
        for c in range(chunks):
            for d in mates:
                push(g_mate[d], own(chunks - 1 - c), 0, d, chunks - 1 - c, at(0, d))
            if c < chunks - side:
                push(g_ahead, own(c), 2, 0, c, at(2, 0))
            else:
                pl.when(even)(lambda: push(g_ahead, own(c), 2, 0, c, at(2, 0), True))
                pl.when(wrap_out)(lambda: push_hop(g_ahead, own(c), c - chunks + 2 * side, at(-2, 0)))
            pl.when(odd)(lambda: push(g_third, own(c), 3, 0, c, at(3, 0)))
        for c in range(chunks):
            pl.when(even)(lambda: push(g_third, own(c), 3, 0, c, at(3, 0), True))

    blk_copy.start()
    col_copy.wait()
    cnt_copy.wait()
    col = col_v[...]
    within = rem(col, per_piece)
    stop = rem(t - div(col, per_piece) + loop_n, loop_n)
    member = rem(m - div(within, tps) + team_n, team_n)
    key = (stop * team_n + member) * tps + rem(within, tps)
    number = lax.broadcasted_iota(jnp.int32, key.shape, 1)
    end = jnp.zeros((1, 1), jnp.int32)
    for r in range(rows_here):
        end = end + cnt_v[:, r:r + 1]
        key = key + jnp.where(number >= end, span, 0)
    key = jnp.where(number < end, key, -1)
    entries = inv_v.shape[1]
    keys = jnp.broadcast_to(key, (LANES, slots)).T[:, :1]
    hit = keys == lax.broadcasted_iota(jnp.int32, (slots, entries), 1)
    owner = jnp.where(hit, lax.broadcasted_iota(jnp.int32, (slots, entries), 0), slots)
    inv_v[...] = jnp.min(owner, axis=0, keepdims=True)
    inv_copy = pltpu.make_async_copy(inv_v, inv_s, loc.at[4])
    inv_copy.start()
    blk[slots] = jnp.zeros(blk.shape[1:], blk.dtype)
    inv_copy.wait()
    blk_copy.wait()

    def product(k, d, c, n):
        total = None
        step = 2 if (n * per_chunk) % 2 == 0 else 1
        for j in range(0, n * per_chunk, step):
            near = c * per_chunk + j
            base = (k * team_n + d) * tps + near
            left = []
            for r in range(rows_here):
                pair = [blk[inv_s[0, r * span + base + i]] for i in range(step)]
                left.append(jnp.concatenate(pair, axis=1))
            start = near * edge if isinstance(near, int) else pl.multiple_of(near * edge, edge)
            part = jnp.dot(jnp.concatenate(left, axis=0), win[k, d, pl.ds(start, step * edge)],
                           preferred_element_type=jnp.float32)
            total = part if total is None else total + part
        return total

    def compute(*parts, n=1):
        total = None
        for k, d, c in parts:
            part = product(k, d, c, n)
            total = part if total is None else total + part
        out_ref[...] += total

    def whole(*parts):
        compute(*((k, d, 0) for k, d in parts), n=chunks)

    out_ref[...] = product(0, 0, 0, chunks)

    def relayed(k, c):
        return c >= chunks // 4, k == 2, c >= chunks - chunks // 2

    def where(flags, is_far, swap):
        masks = (odd, even & ~is_far, even & is_far) if swap else (even, odd & ~is_far, odd & is_far)
        chosen = [mask for mask, flag in zip(masks, flags) if flag]
        if len(chosen) in (0, 3):
            return None if chosen else False
        return functools.reduce(jnp.logical_or, chosen)

    halves = [range(0, (chunks + 1) // 2), range((chunks + 1) // 2, chunks)]
    ends = {run[-1]: run for run in halves if len(run)}

    def upper_core():
        g_low_mate = {d: group() for d in mates}
        g_low_piece = {k: group() for k in (2, 3)}
        g_low_far = {(k, d): group() for k in (2, 3) for d in mates}
        g_third_mate = {d: group(even | wrap_out) for d in mates}
        g_side = group(even & wrap_in)
        g_on, g_over = {}, {}
        for k in (2, 3):
            for c in range(chunks):
                flags = relayed(k, c)
                on = where(flags, wrap_out, False)
                over = where([not flag for flag in flags], wrap_in, True)
                for d in mates:
                    if on is not False:
                        g_on[k, d, c] = group(on, 1)
                    if over is not False:
                        g_over[k, d, c] = group(over, 1)
        late = odd & wrap_out

        def mate(c):
            for d in mates:
                got = arrive(0, d, c)
                if (2, d, c) in g_on:
                    push(g_on[2, d, c], got, 2, d, c, at(2, 0))
                pl.when(even)(lambda: push(g_third_mate[d], got, 3, d, c, at(3, 0), True))
                got = arrive(1, d, c)
                if (3, d, c) in g_on:
                    push(g_on[3, d, c], got, 3, d, c, at(2, 0))
                push(g_low_mate[d], got, 0, d, c, at(-1, 0))

        def piece(k, c):
            got = arrive(k, 0, c)
            for d in mates:
                if (k, d, c) in g_over:
                    push(g_over[k, d, c], got, k, d, c, at(0, d))
            push(g_low_piece[k], got, k - 1, 0, c, at(-1, 0))
            if k == 2:
                push(g_side, got, 3, 0, c, at(1, 0))

        def far(k, d, c):
            got = arrive(k, d, c)
            push(g_low_far[k, d], got, k - 1, d, c, at(-1, 0))

        g_hop = group(hop_here, 2 * side)
        for i, c in enumerate(backward):
            mate(c)
            if i < side:
                @pl.when(hop_here)
                def _():
                    for k in (2, 3):
                        slot = i + (3 - k) * side
                        pltpu.make_async_copy(hop.at[slot], hop.at[slot], hop_recv.at[slot]).wait()
                        push(g_hop, hop.at[slot], k, 0, chunks - side + i, at(4, 0), True)
        for d in mates:
            @pl.when(late)
            def _():
                if d == 1:
                    finish(g_ahead)
                for c in backward:
                    push(g_third_mate[d], win.at[0, d, rows(c)], 3, d, c, at(3, 0), True)

        def early():
            for c in range(chunks):
                arrive(1, 0, c)
            whole((1, 0), *((k, d) for d in mates for k in (0, 1)))

        @pl.when(~(even & wrap_in))
        def _():
            for c in range(chunks):
                piece(3, c)

            @pl.when(odd)
            def _():
                for c in range(chunks):
                    piece(2, c)
            early()

            @pl.when(even)
            def _():
                for c in range(chunks):
                    piece(2, c)
            whole((3, 0), (2, 0))
            for run in halves:
                parts = []
                for i in run:
                    c3 = 0 if i == 0 else jnp.where(odd, chunks - i, i)
                    c2 = jnp.where(odd, 0 if i == 0 else chunks - i, chunks - 1 - i)
                    for d in mates:
                        far(3, d, c3)
                        far(2, d, c2)
                        parts += [(3, d, c3), (2, d, c2)]
                compute(*parts)

        def back_at(i):
            return i if i < chunks - chunks // 2 else 2 * chunks - 1 - chunks // 2 - i

        @pl.when(even & wrap_in)
        def _():
            for s in range(chunks + 2):
                if s < chunks:
                    for k in (2, 3):
                        piece(k, s)
                if s >= 2:
                    for d in mates:
                        for k in (2, 3):
                            far(k, d, back_at(s - 2))
            for c in range(chunks):
                arrive(1, 0, c)
            whole((1, 0), (3, 0), (2, 0), *((k, d) for d in mates for k in range(4)))

    def lower_core():
        g_three = {d: group(odd & ~wrap_in) for d in mates}
        g_back = group(odd & ~wrap_in)

        def mate():
            for d in mates:
                for c in backward:
                    arrive(0, d, c)
                whole((0, d))

        def third(forward):
            for c in range(chunks):
                got = arrive(3, 0, c)
                if forward:
                    push(g_back, got, 2, 0, c, at(-1, 0))
                    for d in mates:
                        push(g_three[d], got, 3, d, c, at(0, d))
            whole((3, 0))

        def third_mate():
            for d in mates:
                for c in backward:
                    arrive(3, d, c)
                whole((3, d))

        def pieces():
            for c in range(chunks):
                for k in (2, 1):
                    arrive(k, 0, c)
            whole((2, 0), (1, 0))

        def fars():
            for run in halves:
                parts = []
                for i in run:
                    c2 = 0 if i == 0 else jnp.where(odd, chunks - i, i)
                    c1 = jnp.where(odd, 0 if i == 0 else chunks - i, chunks - 1 - i)
                    for d in mates:
                        arrive(2, d, c2)
                        arrive(1, d, c1)
                        parts += [(2, d, c2), (1, d, c1)]
                compute(*parts)

        @pl.when(~wrap_in & even)
        def _():
            mate()
            third(False)
            pieces()
            third_mate()
            fars()

        @pl.when(~wrap_in & odd)
        def _():
            third(True)
            mate()
            pieces()
            fars()
            third_mate()

        @pl.when(wrap_in & odd)
        def _():
            mate()
            pieces()
            fars()
            third(False)
            third_mate()

        @pl.when(wrap_in & even)
        def _():
            mate()
            for run in halves:
                parts = [(k, 0, c) for c in run for k in (3, 1, 2)]
                for part in parts:
                    arrive(*part)
                compute(*parts)
            for run in halves:
                parts = []
                for d in mates:
                    for c in run:
                        parts += [(3, d, chunks - 1 - c), (1, d, c), (2, d, c)]
                for part in parts:
                    arrive(*part)
                compute(*parts)

    def role(body):
        mark = len(groups)
        body()
        for g in range(mark, len(groups)):
            finish(g)
        del groups[mark:]

    pl.when(upper)(lambda: role(upper_core))
    pl.when(lower)(lambda: role(lower_core))

    @pl.when(lower | even)
    def _():
        finish(g_ahead)
    for d in mates:
        finish(g_mate[d])
    finish(g_third)


def sends(team_n, chunks):
    mates = team_n - 1
    return 6 + mates * (5 + 4 * chunks)


def in_hbm(x):
    return pltpu.with_memory_space_constraint(x, pltpu.HBM)


def local(loop_n, team_n, blocks, probes, row_count, column_of_slot):
    slots, edge, _ = blocks.shape
    width = probes.shape[1]
    tps = probes.shape[0] // edge
    rows_here = row_count.shape[0]
    chunks = min(4, tps)
    hops = max(1, chunks // 4)
    geo = (loop_n, team_n, chunks, rows_here, slots, edge, tps)
    entries = rows_here * STOPS * team_n * tps
    table = (1, -(-entries // LANES) * LANES)
    return pl.pallas_call(
        functools.partial(kernel, geo),
        out_shape=jax.ShapeDtypeStruct((rows_here * edge, width), jnp.float32),
        in_specs=[pl.BlockSpec(memory_space=pltpu.HBM)] * 4,
        out_specs=pl.BlockSpec(memory_space=pltpu.VMEM),
        scratch_shapes=[
            pltpu.VMEM((slots + 1, edge, edge), blocks.dtype),
            pltpu.VMEM((STOPS, team_n, tps * edge, width), probes.dtype),
            pltpu.VMEM((2 * hops, tps * edge // chunks, width), probes.dtype),
            pltpu.VMEM((1, slots), jnp.int32),
            pltpu.VMEM((1, rows_here), jnp.int32),
            pltpu.VMEM(table, jnp.int32),
            pltpu.SMEM(table, jnp.int32),
            pltpu.SemaphoreType.DMA((STOPS, team_n, chunks)),
            pltpu.SemaphoreType.DMA((2 * hops,)),
            pltpu.SemaphoreType.DMA((sends(team_n, chunks),)),
            pltpu.SemaphoreType.DMA((5,)),
        ],
        compiler_params=pltpu.CompilerParams(
            collective_id=0, has_side_effects=True, vmem_limit_bytes=55000 * 1024),
    )(in_hbm(column_of_slot), in_hbm(row_count), blocks, probes)


def solution(mesh):
    spec = ("loop", "team")
    return jax.shard_map(
        functools.partial(local, mesh.shape["loop"], mesh.shape["team"]),
        mesh=mesh,
        in_specs=(P(spec, None, None), P(spec, None), P(spec), P(spec)),
        out_specs=P(spec, None),
        check_vma=False,
    )
```

```python
import functools

import jax
import jax.numpy as jnp
from jax import lax
from jax.experimental import pallas as pl
from jax.experimental.pallas import tpu as pltpu
from jax.sharding import PartitionSpec as P

STOPS = 4
LANES = 128


def div(x, n):
    return lax.shift_right_logical(x, n.bit_length() - 1) if n & (n - 1) == 0 else lax.div(x, n)


def rem(x, n):
    return x & (n - 1) if n & (n - 1) == 0 else lax.rem(x, n)


def kernel(geo, col_ref, cnt_ref, blocks_ref, probes_ref, out_ref,
           blk, win, hop, col_v, cnt_v, inv_v, inv_s, recv, hop_recv, send, loc):
    loop_n, team_n, chunks, rows_here, slots, edge, tps = geo
    chunk = tps * edge // chunks
    per_chunk = tps // chunks
    per_piece = team_n * tps
    span = STOPS * per_piece
    mates = range(1, team_n)
    t = lax.axis_index("loop")
    m = lax.axis_index("team")
    core = lax.rem(t, 2)
    lower = core == 0
    upper = core == 1
    odd = lax.rem(lax.div(t, 2), 2) == 1
    even = ~odd
    wrap_in = t < 4
    wrap_out = t >= loop_n - 2
    hop_here = t == loop_n - 3
    hop_to = t == 1
    side = max(1, chunks // 4)

    def at(dt, dm):
        return {"loop": lax.rem(t + dt + loop_n, loop_n), "team": lax.rem(m + dm + team_n, team_n)}

    own_copy = pltpu.make_async_copy(probes_ref, win.at[0, 0], loc.at[0])
    col_copy = pltpu.make_async_copy(col_ref, col_v.at[0], loc.at[1])
    cnt_copy = pltpu.make_async_copy(cnt_ref, cnt_v.at[0], loc.at[2])
    blk_copy = pltpu.make_async_copy(blocks_ref, blk.at[pl.ds(0, slots)], loc.at[3])
    own_copy.start()

    barrier = pltpu.get_barrier_semaphore()

    def greet(dt, dm):
        pl.semaphore_signal(barrier, inc=1, device_id=at(dt, dm), device_id_type=pl.DeviceIdType.MESH)

    greet(-3, 0)

    @pl.when(upper)
    def _():
        greet(-2, 0)
        pl.when(even & ~wrap_in)(lambda: greet(1, 0))
        pl.when(hop_here)(lambda: greet(2, 0))
        pl.when(hop_to)(lambda: greet(-4, 0))
        for d in mates:
            greet(-1, d)
            greet(0, d)

    @pl.when(lower & odd)
    def _():
        pl.when(wrap_in)(lambda: greet(-1, 0))
        for d in mates:
            pl.when(~wrap_in)(lambda: greet(0, d))
    greet(1 - 2 * core, 0)

    col_copy.start()
    cnt_copy.start()

    near_odd = (odd & ~wrap_in).astype(jnp.int32)
    far_even = (even & wrap_in).astype(jnp.int32)
    pl.semaphore_wait(barrier, jnp.where(
        lower, team_n + 1 + team_n * near_odd,
        team_n + 2 + far_even + (hop_here | wrap_out).astype(jnp.int32)))

    own_copy.wait()

    groups = []

    def rows(c):
        return pl.ds(c * chunk if isinstance(c, int) else pl.multiple_of(c * chunk, chunk), chunk)

    def group(only=None, size=chunks):
        groups.append((only, size))
        return len(groups) - 1

    def push(g, src, k, d, c, where, always=False):
        copy = pltpu.make_async_remote_copy(
            src_ref=src, dst_ref=win.at[k, d, rows(c)],
            send_sem=send.at[g], recv_sem=recv.at[k, d, c],
            device_id=where, device_id_type=pl.DeviceIdType.MESH)
        if always or groups[g][0] is None:
            copy.start()
        else:
            pl.when(groups[g][0])(copy.start)

    def push_hop(g, src, slot, where):
        pltpu.make_async_remote_copy(
            src_ref=src, dst_ref=hop.at[slot], send_sem=send.at[g], recv_sem=hop_recv.at[slot],
            device_id=where, device_id_type=pl.DeviceIdType.MESH).start()

    def finish(g):
        only, size = groups[g]

        def wait():
            ref = win.at[0, 0, pl.ds(0, size * chunk)]
            pltpu.make_async_copy(ref, ref, send.at[g]).wait()
        if only is None:
            wait()
        else:
            pl.when(only)(wait)

    def arrive(k, d, c):
        ref = win.at[k, d, rows(c)]
        pltpu.make_async_copy(ref, ref, recv.at[k, d, c]).wait()
        return ref

    backward = range(chunks - 1, -1, -1)
    passed = lower | even | wrap_out
    g_ahead = group(passed)
    g_mate = {d: group() for d in mates}
    g_third = group(lower | ~(odd & wrap_out))

    def own(c):
        return win.at[0, 0, rows(c)]

    @pl.when(lower)
    def _():
        for c in range(chunks):
            if c < chunks - side:
                push(g_ahead, own(c), 3, 0, c, at(3, 0))
            else:
                pl.when(~(odd & wrap_out))(lambda: push(g_ahead, own(c), 3, 0, c, at(3, 0), True))
                pl.when(odd & wrap_out)(lambda: push_hop(g_ahead, own(c), c - chunks + side, at(-1, 0)))
            for d in mates:
                push(g_mate[d], own(chunks - 1 - c), 1, d, chunks - 1 - c, at(1, d))
        for c in range(chunks):
            push(g_third, own(c), 1, 0, c, at(1, 0), True)

    @pl.when(upper)
    def _():
        for c in range(chunks):
            if c < chunks - side:
                push(g_ahead, own(c), 2, 0, c, at(2, 0))
            else:
                pl.when(even)(lambda: push(g_ahead, own(c), 2, 0, c, at(2, 0), True))
                pl.when(wrap_out)(lambda: push_hop(g_ahead, own(c), c - chunks + 2 * side, at(-2, 0)))
            for d in mates:
                push(g_mate[d], own(chunks - 1 - c), 0, d, chunks - 1 - c, at(0, d))
            pl.when(odd)(lambda: push(g_third, own(c), 3, 0, c, at(3, 0)))
        for c in range(chunks):
            pl.when(even)(lambda: push(g_third, own(c), 3, 0, c, at(3, 0), True))

    blk_copy.start()
    col_copy.wait()
    cnt_copy.wait()
    col = col_v[...]
    within = rem(col, per_piece)
    stop = rem(t - div(col, per_piece) + loop_n, loop_n)
    member = rem(m - div(within, tps) + team_n, team_n)
    key = (stop * team_n + member) * tps + rem(within, tps)
    number = lax.broadcasted_iota(jnp.int32, key.shape, 1)
    end = jnp.zeros((1, 1), jnp.int32)
    for r in range(rows_here):
        end = end + cnt_v[:, r:r + 1]
        key = key + jnp.where(number >= end, span, 0)
    key = jnp.where(number < end, key, -1)
    entries = inv_v.shape[1]
    keys = jnp.broadcast_to(key, (LANES, slots)).T[:, :1]
    hit = keys == lax.broadcasted_iota(jnp.int32, (slots, entries), 1)
    owner = jnp.where(hit, lax.broadcasted_iota(jnp.int32, (slots, entries), 0), slots)
    inv_v[...] = jnp.min(owner, axis=0, keepdims=True)
    inv_copy = pltpu.make_async_copy(inv_v, inv_s, loc.at[4])
    inv_copy.start()
    blk[slots] = jnp.zeros(blk.shape[1:], blk.dtype)
    inv_copy.wait()
    blk_copy.wait()

    def product(k, d, c, n):
        total = None
        step = 2 if (n * per_chunk) % 2 == 0 else 1
        for j in range(0, n * per_chunk, step):
            near = c * per_chunk + j
            base = (k * team_n + d) * tps + near
            left = []
            for r in range(rows_here):
                pair = [blk[inv_s[0, r * span + base + i]] for i in range(step)]
                left.append(jnp.concatenate(pair, axis=1))
            start = near * edge if isinstance(near, int) else pl.multiple_of(near * edge, edge)
            part = jnp.dot(jnp.concatenate(left, axis=0), win[k, d, pl.ds(start, step * edge)],
                           preferred_element_type=jnp.float32)
            total = part if total is None else total + part
        return total

    def compute(*parts, n=1):
        total = None
        for k, d, c in parts:
            part = product(k, d, c, n)
            total = part if total is None else total + part
        out_ref[...] += total

    def whole(*parts):
        compute(*((k, d, 0) for k, d in parts), n=chunks)

    out_ref[...] = product(0, 0, 0, chunks)

    def relayed(k, c):
        return c >= chunks // 4, k == 2, c >= chunks - chunks // 2

    def where(flags, is_far, swap):
        masks = (odd, even & ~is_far, even & is_far) if swap else (even, odd & ~is_far, odd & is_far)
        chosen = [mask for mask, flag in zip(masks, flags) if flag]
        if len(chosen) in (0, 3):
            return None if chosen else False
        return functools.reduce(jnp.logical_or, chosen)

    halves = [range(0, (chunks + 1) // 2), range((chunks + 1) // 2, chunks)]
    ends = {run[-1]: run for run in halves if len(run)}

    def upper_core():
        g_low_mate = {d: group() for d in mates}
        g_low_piece = {k: group() for k in (2, 3)}
        g_low_far = {(k, d): group() for k in (2, 3) for d in mates}
        g_third_mate = {d: group(even | wrap_out) for d in mates}
        g_side = group(even & wrap_in)
        g_on, g_over = {}, {}
        for k in (2, 3):
            for c in range(chunks):
                flags = relayed(k, c)
                on = where(flags, wrap_out, False)
                over = where([not flag for flag in flags], wrap_in, True)
                for d in mates:
                    if on is not False:
                        g_on[k, d, c] = group(on, 1)
                    if over is not False:
                        g_over[k, d, c] = group(over, 1)
        late = odd & wrap_out

        def mate(c):
            for d in mates:
                got = arrive(0, d, c)
                if (2, d, c) in g_on:
                    push(g_on[2, d, c], got, 2, d, c, at(2, 0))
                pl.when(even)(lambda: push(g_third_mate[d], got, 3, d, c, at(3, 0), True))
                got = arrive(1, d, c)
                if (3, d, c) in g_on:
                    push(g_on[3, d, c], got, 3, d, c, at(2, 0))
                push(g_low_mate[d], got, 0, d, c, at(-1, 0))

        def piece(k, c):
            got = arrive(k, 0, c)
            for d in mates:
                if (k, d, c) in g_over:
                    push(g_over[k, d, c], got, k, d, c, at(0, d))
            push(g_low_piece[k], got, k - 1, 0, c, at(-1, 0))
            if k == 2:
                push(g_side, got, 3, 0, c, at(1, 0))

        def far(k, d, c):
            got = arrive(k, d, c)
            push(g_low_far[k, d], got, k - 1, d, c, at(-1, 0))

        g_hop = group(hop_here, 2 * side)
        for i, c in enumerate(backward):
            mate(c)
            if i < side:
                @pl.when(hop_here)
                def _():
                    for k in (2, 3):
                        slot = i + (3 - k) * side
                        pltpu.make_async_copy(hop.at[slot], hop.at[slot], hop_recv.at[slot]).wait()
                        push(g_hop, hop.at[slot], k, 0, chunks - side + i, at(4, 0), True)
        for d in mates:
            @pl.when(late)
            def _():
                if d == 1:
                    finish(g_ahead)
                for c in backward:
                    push(g_third_mate[d], win.at[0, d, rows(c)], 3, d, c, at(3, 0), True)

        def early():
            for c in range(chunks):
                arrive(1, 0, c)
            whole((1, 0), *((k, d) for d in mates for k in (0, 1)))

        @pl.when(~(even & wrap_in))
        def _():
            for c in range(chunks):
                piece(3, c)

            @pl.when(odd)
            def _():
                for c in range(chunks):
                    piece(2, c)
            early()

            @pl.when(even)
            def _():
                for c in range(chunks):
                    piece(2, c)
            whole((3, 0), (2, 0))
            for run in halves:
                parts = []
                for i in run:
                    c3 = 0 if i == 0 else jnp.where(odd, chunks - i, i)
                    c2 = jnp.where(odd, 0 if i == 0 else chunks - i, chunks - 1 - i)
                    for d in mates:
                        far(3, d, c3)
                        far(2, d, c2)
                        parts += [(3, d, c3), (2, d, c2)]
                compute(*parts)

        def back_at(i):
            return i if i < chunks - chunks // 2 else 2 * chunks - 1 - chunks // 2 - i

        @pl.when(even & wrap_in)
        def _():
            for s in range(chunks + 2):
                if s < chunks:
                    for k in (2, 3):
                        piece(k, s)
                if s >= 2:
                    for d in mates:
                        for k in (2, 3):
                            far(k, d, back_at(s - 2))
            for c in range(chunks):
                arrive(1, 0, c)
            whole((1, 0), (3, 0), (2, 0), *((k, d) for d in mates for k in range(4)))

    def lower_core():
        g_three = {d: group(odd & ~wrap_in) for d in mates}
        g_back = group(odd & ~wrap_in)

        def mate():
            for d in mates:
                for c in backward:
                    arrive(0, d, c)
                whole((0, d))

        def third(forward):
            for c in range(chunks):
                got = arrive(3, 0, c)
                if forward:
                    push(g_back, got, 2, 0, c, at(-1, 0))
                    for d in mates:
                        push(g_three[d], got, 3, d, c, at(0, d))
            whole((3, 0))

        def third_mate():
            for d in mates:
                for c in backward:
                    arrive(3, d, c)
                whole((3, d))

        def pieces():
            for c in range(chunks):
                for k in (2, 1):
                    arrive(k, 0, c)
            whole((2, 0), (1, 0))

        def fars():
            for run in halves:
                parts = []
                for i in run:
                    c2 = 0 if i == 0 else jnp.where(odd, chunks - i, i)
                    c1 = jnp.where(odd, 0 if i == 0 else chunks - i, chunks - 1 - i)
                    for d in mates:
                        arrive(2, d, c2)
                        arrive(1, d, c1)
                        parts += [(2, d, c2), (1, d, c1)]
                compute(*parts)

        @pl.when(~wrap_in & even)
        def _():
            mate()
            third(False)
            pieces()
            third_mate()
            fars()

        @pl.when(~wrap_in & odd)
        def _():
            third(True)
            mate()
            pieces()
            fars()
            third_mate()

        @pl.when(wrap_in & odd)
        def _():
            mate()
            pieces()
            fars()
            third(False)
            third_mate()

        @pl.when(wrap_in & even)
        def _():
            mate()
            for run in halves:
                parts = [(k, 0, c) for c in run for k in (3, 1, 2)]
                for part in parts:
                    arrive(*part)
                compute(*parts)
            for run in halves:
                parts = []
                for d in mates:
                    for c in run:
                        parts += [(3, d, chunks - 1 - c), (1, d, c), (2, d, c)]
                for part in parts:
                    arrive(*part)
                compute(*parts)

    def role(body):
        mark = len(groups)
        body()
        for g in range(mark, len(groups)):
            finish(g)
        del groups[mark:]

    pl.when(upper)(lambda: role(upper_core))
    pl.when(lower)(lambda: role(lower_core))

    @pl.when(lower | even)
    def _():
        finish(g_ahead)
    for d in mates:
        finish(g_mate[d])
    finish(g_third)


def sends(team_n, chunks):
    mates = team_n - 1
    return 6 + mates * (5 + 4 * chunks)


def in_hbm(x):
    return pltpu.with_memory_space_constraint(x, pltpu.HBM)


def local(loop_n, team_n, blocks, probes, row_count, column_of_slot):
    slots, edge, _ = blocks.shape
    width = probes.shape[1]
    tps = probes.shape[0] // edge
    rows_here = row_count.shape[0]
    chunks = min(4, tps)
    hops = max(1, chunks // 4)
    geo = (loop_n, team_n, chunks, rows_here, slots, edge, tps)
    entries = rows_here * STOPS * team_n * tps
    table = (1, -(-entries // LANES) * LANES)
    return pl.pallas_call(
        functools.partial(kernel, geo),
        out_shape=jax.ShapeDtypeStruct((rows_here * edge, width), jnp.float32),
        in_specs=[pl.BlockSpec(memory_space=pltpu.HBM)] * 4,
        out_specs=pl.BlockSpec(memory_space=pltpu.VMEM),
        scratch_shapes=[
            pltpu.VMEM((slots + 1, edge, edge), blocks.dtype),
            pltpu.VMEM((STOPS, team_n, tps * edge, width), probes.dtype),
            pltpu.VMEM((2 * hops, tps * edge // chunks, width), probes.dtype),
            pltpu.VMEM((1, slots), jnp.int32),
            pltpu.VMEM((1, rows_here), jnp.int32),
            pltpu.VMEM(table, jnp.int32),
            pltpu.SMEM(table, jnp.int32),
            pltpu.SemaphoreType.DMA((STOPS, team_n, chunks)),
            pltpu.SemaphoreType.DMA((2 * hops,)),
            pltpu.SemaphoreType.DMA((sends(team_n, chunks),)),
            pltpu.SemaphoreType.DMA((5,)),
        ],
        compiler_params=pltpu.CompilerParams(
            collective_id=0, has_side_effects=True, vmem_limit_bytes=55000 * 1024),
    )(in_hbm(column_of_slot), in_hbm(row_count), blocks, probes)


def solution(mesh):
    spec = ("loop", "team")
    return jax.shard_map(
        functools.partial(local, mesh.shape["loop"], mesh.shape["team"]),
        mesh=mesh,
        in_specs=(P(spec, None, None), P(spec, None), P(spec), P(spec)),
        out_specs=P(spec, None),
        check_vma=False,
    )
```
